32 devices in a mesh: groups: 2 (over x), slab: 16 (over z, y, core).
Axes of the slice: x: 2, y: 2, z: 4, core: 2. Of those that a mesh axis runs over, the one named last changes fastest.
Arguments:
- latents: bfloat16 [32768, 512], P(('groups', 'slab')), parts along dimension 0, may hold values from -6 to 6
- positions: float32 [3, 32768], P(None, ('groups', 'slab')), parts along dimension 1, may hold values from -5 to 5
- counts: int32 [32], P(('groups', 'slab')), parts along dimension 0, may hold values from 1 to 1024, 12288 in all
- send_rows: int32 [32, 2, 256], P(('groups', 'slab')), parts along dimension 0, may hold values from 0 to 1023, as said below
- tiles: int32 [32, 8, 4], P(('groups', 'slab')), parts along dimension 0, may hold values from 0 to 11, as said below
- w_msg: bfloat16 [2, 512, 512], replicated, may hold values from -0.25 to 0.25
- w_in: bfloat16 [2, 2, 512, 1024], replicated, may hold values from -0.1875 to 0.1875
- w_out: bfloat16 [2, 1024, 512], replicated, may hold values from -0.1875 to 0.1875
- cotangent: bfloat16 [32768, 512], P(('groups', 'slab')), parts along dimension 0, may hold values from -6 to 6
Outputs:
- final_latents: bfloat16 [32768, 512], P(('groups', 'slab')), parts along dimension 0
- grad_latents: float32 [32768, 512], P(('groups', 'slab')), parts along dimension 0
- grad_msg: float32 [4, 512, 512], P('groups', 'slab'), parts along dimension 0
- grad_in: float32 [4, 2, 512, 1024], P('groups', None, 'slab'), parts along dimension 0
- grad_out: float32 [4, 1024, 512], P('groups', 'slab'), parts along dimension 0
The draws below stay inside these ranges and needn't reach their ends.
There are 2 independent parts, one for each index of `groups`. The reference program is written for one: setup_inputs(seed, part) draws one part's arguments, and reference() takes and returns one part's arrays. A program takes and returns all parts, laid end to end along the dimension named above; an argument that names none is the same for every part. Nothing has to cross between parts.
Inputs may be any that keep to these rules, and one draw needn't show every extreme that they name: Each list send_rows[s, d] holds 256 different rows and always includes rows 0 and 1023. tiles[s, t, 0] = t + 2; the 4 entries of a row differ; the first local tile lists extended tile 0 and the last local tile lists the last extended tile.
All inputs are finite; a program needn't handle non-finite values. No bound on the sum of `counts` on one device may be relied on, other than what follows from the above.
Results may differ from the reference program's by a relative error of at most 0.025.
Values may be sent and summed in bfloat16 or wider, within the bound.
No kernel may reach another device: no remote copies, remote signals or barrier semaphores. Data moves between devices by JAX's collectives and lax.ppermute only.
A program may use at most 128 MiB of HBM per device.

```python
import math
import jax
import jax.numpy as jnp
import numpy as np
from jax import lax

L = 512
H = 1024
LAYERS = 2
TILE = 128
K = 4
HALO = 256
P_DEV = 1024
NP = 16384
N_SLAB = 16


def draw_send_rows(key, part):
    keys = jax.random.split(key, N_SLAB * 2)

    def one_list(list_key):
        inner = jax.random.permutation(list_key, P_DEV - 2).astype(jnp.int32) + 1
        ends = jnp.array([0, P_DEV - 1], jnp.int32)
        return jnp.concatenate([ends, inner[:HALO - 2]])
    return jax.vmap(one_list)(keys).reshape(N_SLAB, 2, HALO).astype(jnp.int32)


def draw_tiles(key, part):
    tile_count = P_DEV // TILE
    ghost_tiles = HALO // TILE
    ext_count = tile_count + 2 * ghost_tiles
    noise = jax.random.randint(key, (N_SLAB, tile_count, ext_count), 0, 16).astype(jnp.int32)
    mine = jnp.arange(tile_count, dtype=jnp.int32)[:, None] + ghost_tiles
    candidate = jnp.arange(ext_count, dtype=jnp.int32)[None, :]
    score = jnp.abs(candidate - mine) * 8 + noise
    score = jnp.where(candidate == mine, -2, score)
    score = jnp.where((mine == ghost_tiles) & (candidate == 0), -1, score)
    score = jnp.where((mine == ghost_tiles + tile_count - 1) & (candidate == ext_count - 1), -1, score)
    score = score * ext_count + candidate
    order = jnp.argsort(score, axis=-1, stable=True)
    return order[..., :K].astype(jnp.int32)


def block_scale(rng, dims, cuts, low, high):
    level, own = 1.0, jax.random.fold_in(rng, 6)
    for axis_at, blocks in cuts:
        steps = jnp.exp(jax.random.uniform(jax.random.fold_in(own, axis_at), (blocks,), jnp.float32, low / len(cuts), high / len(cuts)))
        level = level * jnp.repeat(steps, dims[axis_at] // blocks).reshape([-1 if axis == axis_at else 1 for axis in range(len(dims))])
    return level


def length_profile(number_of, total, limit, lean):
    weights = [(1 << 20) // math.isqrt(grade ** lean) + 1 for grade in range(2, number_of + 1)]
    rest, holding = total - limit - (number_of - 1), [1] * (number_of - 1)
    while rest > 0:
        movable = [i for i in range(number_of - 1) if holding[i] < limit]
        pool, remaining = sum([weights[i] for i in movable]), rest
        for i in movable:
            addition = min(limit - holding[i], max(1, remaining * weights[i] // pool), rest)
            holding[i] = holding[i] + addition
            rest = rest - addition
    return np.array([limit] + holding)


def ragged_sizes(own_key, number_of, total, limit, slope):
    if number_of == 2:
        one = jax.random.randint(own_key, (), max(1, total - limit), min(limit, total - 1) + 1)
        return jnp.stack([one, total - one])
    tallies = jnp.asarray(length_profile(number_of, total, limit, slope), jnp.int32)
    twos = (number_of - 1) // 2
    giver, taker = tallies[1:1 + 2 * twos:2], tallies[2:2 + 2 * twos:2]
    room = jnp.minimum(giver - 1, limit - taker)
    moved = jax.random.randint(jax.random.fold_in(own_key, 1), (twos,), 0, 1 << 20) % (room + 1)
    tallies = tallies.at[1:1 + 2 * twos:2].set(giver - moved).at[2:2 + 2 * twos:2].set(taker + moved)
    return tallies[jax.random.permutation(jax.random.fold_in(own_key, 2), number_of)]


def bell_draw(own_key, dims, deviation, limit, cuts=(), kind=jnp.bfloat16):
    level = block_scale(own_key, dims, cuts, -0.22, 0.18) if cuts else 1.0
    values = jax.random.normal(own_key, dims, jnp.float32) * deviation * level
    return jnp.minimum(jnp.maximum(values, -limit), limit).astype(kind)


def setup_inputs(seed: int = 0, part: int = 0) -> dict:
    key_list = jax.random.split(jax.random.key(seed), 10)
    own_keys = jax.random.split(jax.random.fold_in(key_list[9], part), 10)
    latents = bell_draw(own_keys[0], (NP, L), 1.0, 6.0, ((0, 16),))
    positions = bell_draw(own_keys[1], (3, NP), 1.0, 5.0, ((1, 16),), jnp.float32)
    counts = ragged_sizes(own_keys[2], N_SLAB, 3 * P_DEV * N_SLAB // 4, P_DEV, 2).astype(jnp.int32)
    send_rows = draw_send_rows(jax.random.fold_in(jax.random.fold_in(key_list[9], part), 71), part)
    tiles = draw_tiles(jax.random.fold_in(jax.random.fold_in(key_list[9], part), 71), part)
    w_msg = bell_draw(key_list[5], (LAYERS, L, L), L ** -0.5, 0.25)
    w_in = bell_draw(key_list[6], (LAYERS, 2, L, H), (2 * L) ** -0.5, 0.1875)
    w_out = bell_draw(key_list[7], (LAYERS, H, L), H ** -0.5, 0.1875)
    cotangent = bell_draw(own_keys[8], (NP, L), 1.0, 6.0, ((0, 16),))
    return {"latents": latents, "positions": positions, "counts": counts, "send_rows": send_rows, "tiles": tiles, "w_msg": w_msg, "w_in": w_in, "w_out": w_out, "cotangent": cotangent}


def take_rows(block, index):
    return jax.vmap(lambda slab_rows, picked: slab_rows[picked])(block, index)

def with_ghosts(block, send_rows):
    to_lower = take_rows(block, send_rows[:, 0])
    to_upper = take_rows(block, send_rows[:, 1])
    blank = jnp.zeros_like(to_lower[:1])
    from_lower = jnp.concatenate([blank, to_upper[:-1]], axis=0)
    from_upper = jnp.concatenate([to_lower[1:], blank], axis=0)
    return jnp.concatenate([from_lower, block, from_upper], axis=1)

def add_back(own_rows, up_index, up_terms, down_index, down_terms):
    return own_rows.at[up_index].add(up_terms).at[down_index].add(down_terms)

def return_ghosts(extended, send_rows):
    own_count = extended.shape[1] - 2 * HALO
    inner = extended[:, HALO:HALO + own_count]
    lower_part = extended[:, :HALO]
    upper_part = extended[:, HALO + own_count:]
    blank = jnp.zeros_like(lower_part[:1])
    from_above = jnp.concatenate([lower_part[1:], blank], axis=0)
    from_below = jnp.concatenate([blank, upper_part[:-1]], axis=0)
    return jax.vmap(add_back)(inner, send_rows[:, 1], from_above, send_rows[:, 0], from_below)

def kernel(geometry_ext, neighbours):
    tile_count = neighbours.shape[0]
    pieces = geometry_ext.reshape(4, -1, TILE)
    ghost_tiles = (pieces.shape[1] - tile_count) // 2
    mine = pieces[:3, ghost_tiles:ghost_tiles + tile_count]
    nearby = pieces[:, neighbours]
    offset = mine[:, :, None, :, None] - nearby[:3, :, :, None, :]
    distance = lax.optimization_barrier(jnp.sum(offset * offset, axis=0))
    weight = nearby[3][:, :, None, :] / (1.0 + distance)
    scale = jnp.sqrt(1.0 + lax.optimization_barrier(jnp.sum(weight * weight, axis=(1, 3)))).reshape(-1)
    return (weight.astype(jnp.bfloat16), scale)

def gather_message(weight, scale, update_ext, neighbours):
    blocks = update_ext.reshape(-1, TILE, update_ext.shape[-1])[neighbours]
    total = jnp.einsum('tkij,tkjl->til', weight.astype(jnp.float32), blocks.astype(jnp.float32))
    return (total.reshape(-1, update_ext.shape[-1]) / scale[:, None]).astype(jnp.bfloat16)

def spread_message(weight, scale, grad_message, neighbours):
    width = grad_message.shape[-1]
    scaled = (grad_message / scale[:, None]).astype(jnp.bfloat16)
    parts = jnp.einsum('tkij,til->tkjl', weight.astype(jnp.float32), scaled.reshape(-1, TILE, width).astype(jnp.float32))
    ext_tiles = neighbours.shape[0] + 2 * (HALO // TILE)
    total = jnp.zeros((ext_tiles, TILE, width), jnp.float32).at[neighbours].add(parts)
    return total.reshape(-1, width)

def reference(latents, positions, counts, send_rows, tiles, w_msg, w_in, w_out, cotangent):
    f32 = jnp.float32
    bf16 = jnp.bfloat16
    current = latents.reshape(N_SLAB, P_DEV, L)
    alive = (jnp.arange(P_DEV, dtype=jnp.int32)[None, :] < counts[:, None]).astype(f32)
    geometry = jnp.concatenate([positions.reshape(3, N_SLAB, P_DEV).transpose(1, 0, 2), alive[:, None, :]], axis=1)
    geometry_ext = with_ghosts(geometry.transpose(0, 2, 1), send_rows).transpose(0, 2, 1)
    weights, scales = jax.vmap(kernel)(geometry_ext, tiles)
    stored = []
    for layer_idx in range(LAYERS):
        update = jnp.einsum('spl,lm->spm', current.astype(f32), w_msg[layer_idx].astype(f32)).astype(bf16)
        update_ext = with_ghosts(update, send_rows)
        message = jax.vmap(gather_message)(weights, scales, update_ext, tiles)
        pre = jnp.einsum('spl,lk->spk', current.astype(f32), w_in[layer_idx, 0].astype(f32))
        pre = pre + jnp.einsum('spl,lk->spk', message.astype(f32), w_in[layer_idx, 1].astype(f32))
        hidden = jax.nn.silu(pre).astype(bf16)
        delta = jnp.einsum('spk,kl->spl', hidden.astype(f32), w_out[layer_idx].astype(f32))
        stored.append((current, message, pre, hidden))
        current = (current.astype(f32) + alive[:, :, None] * delta).astype(bf16)
    norm_scale = 1.0 / jnp.sqrt(jnp.asarray(N_SLAB * P_DEV, f32))
    gradient = cotangent.astype(f32).reshape(N_SLAB, P_DEV, L)
    msg_terms = [None] * LAYERS
    in_terms = [None] * LAYERS
    out_terms = [None] * LAYERS
    for layer_idx in reversed(range(LAYERS)):
        before, message, pre, hidden = stored[layer_idx]
        grad_delta = (alive[:, :, None] * gradient).astype(bf16)
        out_terms[layer_idx] = jnp.einsum('spk,spl->kl', hidden.astype(f32), grad_delta.astype(f32))
        grad_hidden = jnp.einsum('spl,kl->spk', grad_delta.astype(f32), w_out[layer_idx].astype(f32))
        sigma = jax.nn.sigmoid(pre)
        grad_pre = (grad_hidden * sigma * (1.0 + pre * (1.0 - sigma))).astype(bf16)
        in_terms[layer_idx] = jnp.stack([jnp.einsum('spl,spk->lk', before.astype(f32), grad_pre.astype(f32)), jnp.einsum('spl,spk->lk', message.astype(f32), grad_pre.astype(f32))])
        direct = jnp.einsum('spk,lk->spl', grad_pre.astype(f32), w_in[layer_idx, 0].astype(f32))
        grad_message = jnp.einsum('spk,lk->spl', grad_pre.astype(f32), w_in[layer_idx, 1].astype(f32))
        grad_ext = jax.vmap(spread_message)(weights, scales, grad_message, tiles)
        grad_update = return_ghosts(grad_ext, send_rows).astype(bf16)
        msg_terms[layer_idx] = jnp.einsum('spl,spm->lm', before.astype(f32), grad_update.astype(f32))
        gradient = gradient + direct + jnp.einsum('spm,lm->spl', grad_update.astype(f32), w_msg[layer_idx].astype(f32))
    grad_msg = jnp.stack(msg_terms) * norm_scale
    grad_in = jnp.stack(in_terms) * norm_scale
    grad_out = jnp.stack(out_terms) * norm_scale
    return (current.reshape(N_SLAB * P_DEV, L), gradient.reshape(N_SLAB * P_DEV, L), grad_msg, grad_in, grad_out)
```

```python
import functools
import math

import jax
import jax.numpy as jnp
from jax import lax
from jax.experimental import pallas as pl
from jax.experimental.pallas import tpu as pltpu
from jax.sharding import PartitionSpec as P

LAYERS = 2
TILE = 128
HALO = 256
GEO = 16
BLOCK = 256
GHOST_TILES = HALO // TILE
F32 = jnp.float32
BF16 = jnp.bfloat16


def dg(a, b, ca, cb):
    return lax.dot_general(a, b, (((ca,), (cb,)), ((), ())), preferred_element_type=F32)


def blocks(n):
    return [slice(r, r + BLOCK) for r in range(0, n, BLOCK)]


def alive_rows(count_ref, rows, start=0):
    index = lax.broadcasted_iota(jnp.int32, (rows, 1), 0) + start
    return jnp.where(index < count_ref[0], 1.0, 0.0).astype(F32)


def picks(rows_ref, d, n):
    index = lax.broadcasted_iota(jnp.int32, (n, HALO), 0)
    return jnp.where(index == rows_ref[d : d + 1, :], 1.0, 0.0).astype(BF16)


def fetch(pairs, sems):
    copies = [pltpu.make_async_copy(src, dst, sems.at[i]) for i, (src, dst) in enumerate(pairs)]
    for copy in copies:
        copy.start()
    return copies


def send_kernel(count, rows, latents, positions, up, down, geo):
    n = latents.shape[0]
    x = positions[...]
    high = x.astype(BF16).astype(F32)
    rest = x - high
    middle = rest.astype(BF16).astype(F32)
    geo[...] = jnp.zeros_like(geo)
    geo[0:3, :] = high
    geo[3:6, :] = middle
    geo[6:9, :] = rest - middle
    lane = lax.broadcasted_iota(jnp.int32, (1, n), 1)
    geo[9:10, :] = jnp.where(lane < count[0], 1.0, 0.0).astype(F32)
    fields = geo[...].astype(BF16)
    for d, out in ((0, down), (1, up)):
        pick = picks(rows, d, n)
        out[0:HALO, :] = dg(pick, latents[...], 0, 0).astype(BF16)
        out[HALO : HALO + GEO, :] = jnp.zeros((GEO, out.shape[1]), BF16)
        out[HALO : HALO + GEO, 0:HALO] = dg(fields, pick, 1, 0).astype(BF16)


def pair_weight(x_column, geo):
    total = None
    for c in range(3):
        offset = x_column[:, c : c + 1] - geo[c : c + 1, :]
        total = offset * offset if total is None else total + offset * offset
    return geo[3:4, :] / (1.0 + total)


def own_kernel(
    count, tiles, latents, positions, cotangent, w_msg, w_in, w_out,
    a_own, squares, columns, update, partial, pre_part, grad_hidden,
    wm, wi, wo, wide, geo, sems,
):
    n = latents.shape[0]
    tile_count = n // TILE
    copies = fetch(((w_msg.at[0], wm), (w_in.at[0, 0], wi), (w_out.at[LAYERS - 1], wo)), sems)
    wide[...] = jnp.zeros_like(wide)
    wide[0:3, :] = positions[...]
    lane = lax.broadcasted_iota(jnp.int32, (1, n), 1)
    wide[3:4, :] = jnp.where(lane < count[0], 1.0, 0.0).astype(F32)
    for t in range(tile_count):
        part = wide[:, t * TILE : (t + 1) * TILE]
        geo[t] = part[0:8]
        columns[t * TILE : (t + 1) * TILE, :] = part.T
    a_own[...] = jnp.zeros_like(a_own)
    squares[...] = jnp.zeros_like(squares)

    def tile_step(t, _):
        rows = pl.ds(pl.multiple_of(t * TILE, TILE), TILE)
        for k in range(tiles.shape[1]):
            near = tiles[t, k] - GHOST_TILES

            @pl.when((near >= 0) & (near < tile_count))
            def _():
                weight = pair_weight(columns[rows, :], geo[near])
                squares[rows, :] += weight * weight
                a_own[rows, pl.ds(pl.multiple_of(near * TILE, TILE), TILE)] = weight.astype(BF16)

        return 0

    lax.fori_loop(0, tile_count, tile_step, 0)
    copies[0].wait()
    update[...] = dg(latents[...], wm[...], 1, 0).astype(BF16)
    partial[...] = dg(a_own[...], update[...], 1, 0)
    copies[1].wait()
    pre_part[...] = dg(latents[...], wi[...], 1, 0).astype(BF16)
    copies[2].wait()
    grad_delta = (cotangent[...].astype(F32) * alive_rows(count, n)).astype(BF16)
    grad_hidden[...] = dg(grad_delta, wo[...], 1, 1).astype(BF16)


def first_kernel(
    count, tiles, rows, latents, lower, upper, squares, columns, partial, pre_part, w_msg, w_in, w_out,
    a_ghost, inverse, message, hidden, slope, current, update, up, down,
    wm, wi, wo, wn, geo, sums, sems,
):
    n = latents.shape[0]
    tile_count = n // TILE
    copies = fetch(
        ((w_msg.at[0], wm), (w_in.at[0, 1], wi), (w_out.at[0], wo), (w_msg.at[1], wn)), sems
    )
    for side, ghost in enumerate((lower, upper)):
        fields = ghost[HALO : HALO + GEO, :].astype(F32)
        place = fields[0:3] + fields[3:6] + fields[6:9]
        for g in range(GHOST_TILES):
            cut = slice(g * TILE, (g + 1) * TILE)
            geo[side * GHOST_TILES + g, 0:3, :] = place[:, cut]
            geo[side * GHOST_TILES + g, 3:4, :] = fields[9:10, cut]
    a_ghost[...] = jnp.zeros_like(a_ghost)
    sums[...] = squares[...]

    def tile_step(t, _):
        own = pl.ds(pl.multiple_of(t * TILE, TILE), TILE)
        for k in range(tiles.shape[1]):
            index = tiles[t, k]
            near = jnp.where(index < GHOST_TILES, index, index - tile_count)

            @pl.when((index < GHOST_TILES) | (index >= GHOST_TILES + tile_count))
            def _():
                weight = pair_weight(columns[own, :], geo[near])
                sums[own, :] += weight * weight
                a_ghost[own, pl.ds(pl.multiple_of(near * TILE, TILE), TILE)] = weight.astype(BF16)

        return 0

    lax.fori_loop(0, tile_count, tile_step, 0)
    copies[0].wait()
    update_lower = dg(lower[0:HALO, :], wm[...], 1, 0).astype(BF16)
    update_upper = dg(upper[0:HALO, :], wm[...], 1, 0).astype(BF16)
    for copy in copies[1:]:
        copy.wait()
    for r in blocks(n):
        inv = 1.0 / jnp.sqrt(1.0 + jnp.sum(sums[r, :], axis=1, keepdims=True))
        inverse[r, :] = jnp.broadcast_to(inv, (BLOCK, TILE))
        total = partial[r, :] + dg(a_ghost[r, 0:HALO], update_lower, 1, 0)
        total = total + dg(a_ghost[r, HALO : 2 * HALO], update_upper, 1, 0)
        mess = (total * inv).astype(BF16)
        message[r, :] = mess
        pre = pre_part[r, :].astype(F32) + dg(mess, wi[...], 1, 0)
        sigma = 1.0 / (1.0 + jnp.exp(-pre))
        hid = (pre * sigma).astype(BF16)
        hidden[r, :] = hid
        slope[r, :] = (sigma * (1.0 + pre * (1.0 - sigma))).astype(BF16)
        delta = dg(hid, wo[...], 1, 0)
        live = alive_rows(count, BLOCK, r.start)
        cur = (latents[r, :].astype(F32) + live * delta).astype(BF16)
        current[r, :] = cur
        update[r, :] = dg(cur, wn[...], 1, 0).astype(BF16)
    down[...] = dg(picks(rows, 0, n), update[...], 0, 0).astype(BF16)
    up[...] = dg(picks(rows, 1, n), update[...], 0, 0).astype(BF16)


def middle_kernel(current, update, a_own, w_in, partial, pre_part, wi, sems):
    copies = fetch(((w_in.at[1, 0], wi),), sems)
    partial[...] = dg(a_own[...], update[...], 1, 0)
    copies[0].wait()
    pre_part[...] = dg(current[...], wi[...], 1, 0).astype(BF16)


def last_kernel(
    lower, upper, a_ghost, inverse, partial, pre_part, grad_hidden, w_in,
    message, hidden, grad_pre, scaled, back_lower, back_upper,
    wi, sems,
):
    n = partial.shape[0]
    copies = fetch(((w_in.at[1, 1], wi),), sems)
    copies[0].wait()
    for r in blocks(n):
        inv = inverse[r, 0:1]
        total = partial[r, :] + dg(a_ghost[r, 0:HALO], lower[...], 1, 0)
        total = total + dg(a_ghost[r, HALO : 2 * HALO], upper[...], 1, 0)
        mess = (total * inv).astype(BF16)
        message[r, :] = mess
        pre = pre_part[r, :].astype(F32) + dg(mess, wi[...], 1, 0)
        sigma = 1.0 / (1.0 + jnp.exp(-pre))
        hidden[r, :] = (pre * sigma).astype(BF16)
        slope = sigma * (1.0 + pre * (1.0 - sigma))
        gpre = (grad_hidden[r, :].astype(F32) * slope).astype(BF16)
        grad_pre[r, :] = gpre
        scaled[r, :] = (dg(gpre, wi[...], 1, 1) * inv).astype(BF16)
    back_lower[...] = dg(a_ghost[:, 0:HALO], scaled[...], 0, 0).astype(BF16)
    back_upper[...] = dg(a_ghost[:, HALO : 2 * HALO], scaled[...], 0, 0).astype(BF16)


def order(count):
    rest = count // 4
    return [(s, ((s % 2) * 2 + (s // 2) % 2) * rest + s // 4) for s in range(count)]


def pack_rows(out, at, term, count):
    rows, width = term.shape[0] // count, out.shape[-1]
    for h in range(term.shape[1] // width):
        for s, place in order(count):
            out[place, at : at + rows, :] = term[s * rows : (s + 1) * rows, h * width : (h + 1) * width]
        at += rows
    return at


def terms_kernel(
    with_final, slabs, norm, *refs,
):
    if with_final:
        (count, before, message, hidden, grad_pre, scaled, grad_in_vec, a_own, w_in, w_out,
         grad_own, direct, packed, final, wi, wo, term, sems) = refs
    else:
        (count, before, message, hidden, grad_pre, scaled, grad_in_vec, later, later_update, a_own, w_in,
         grad_own, direct, packed, wi, term, sems) = refs
    n, width = before.shape
    layer = 1 if with_final else 0
    pairs = [(w_in.at[layer, 0], wi)]
    if with_final:
        pairs.append((w_out.at[layer], wo))
    copies = fetch(pairs, sems)
    live = alive_rows(count, n)
    grad_delta = (grad_in_vec[...].astype(F32) * live).astype(BF16)
    at = 0
    if not with_final:
        value = dg(later[...], later_update[...], 0, 0)
        at = pack_rows(packed, at, (value * norm).astype(BF16), slabs)
    value = dg(hidden[...], grad_delta, 0, 0)
    at = pack_rows(packed, at, (value * norm).astype(BF16), slabs)
    for left in (before, message):
        value = dg(left[...], grad_pre[...], 0, 0)
        at = pack_rows(packed, at, (value * norm).astype(BF16), slabs)
    grad_own[...] = dg(a_own[...], scaled[...], 0, 0)
    copies[0].wait()
    direct[...] = grad_in_vec[...].astype(F32) + dg(grad_pre[...], wi[...], 1, 1)
    if with_final:
        copies[1].wait()
        delta = dg(hidden[...], wo[...], 1, 0)
        final[...] = (before[...].astype(F32) + live * delta).astype(BF16)


def turn_kernel(
    count, rows, grad_own, from_above, from_below, direct, slope, inverse, a_ghost, w_msg, w_in, w_out,
    grad_update, gradient, grad_pre, scaled, back_lower, back_upper,
    wm, wi, wo, sems,
):
    n = direct.shape[0]
    copies = fetch(((w_msg.at[1], wm), (w_out.at[0], wo), (w_in.at[0, 1], wi)), sems)
    pick_down = picks(rows, 0, n)
    pick_up = picks(rows, 1, n)
    for copy in copies:
        copy.wait()
    for r in blocks(n):
        total = grad_own[r, :] + dg(pick_up[r, :], from_above[...], 1, 0)
        total = total + dg(pick_down[r, :], from_below[...], 1, 0)
        gup = total.astype(BF16)
        grad_update[r, :] = gup
        grad = direct[r, :] + dg(gup, wm[...], 1, 1)
        gradient[r, :] = grad
        gdelta = (grad * alive_rows(count, BLOCK, r.start)).astype(BF16)
        gpre = (dg(gdelta, wo[...], 1, 1) * slope[r, :].astype(F32)).astype(BF16)
        grad_pre[r, :] = gpre
        scaled[r, :] = (dg(gpre, wi[...], 1, 1) * inverse[r, 0:1]).astype(BF16)
    back_lower[...] = dg(a_ghost[:, 0:HALO], scaled[...], 0, 0).astype(BF16)
    back_upper[...] = dg(a_ghost[:, HALO : 2 * HALO], scaled[...], 0, 0).astype(BF16)


def end_kernel(
    slabs, norm, rows, grad_own, from_above, from_below, direct, latents, w_msg,
    gradient, packed, wm, gup_all, sems,
):
    n = direct.shape[0]
    copies = fetch(((w_msg.at[0], wm),), sems)
    pick_down = picks(rows, 0, n)
    pick_up = picks(rows, 1, n)
    total = grad_own[...] + dg(pick_up, from_above[...], 1, 0)
    total = total + dg(pick_down, from_below[...], 1, 0)
    gup_all[...] = total.astype(BF16)
    value = dg(latents[...], gup_all[...], 0, 0)
    pack_rows(packed, 0, (value * norm).astype(BF16), slabs)
    copies[0].wait()
    gradient[...] = direct[...] + dg(gup_all[...], wm[...], 1, 1)


VMEM = pl.BlockSpec(memory_space=pltpu.VMEM)
SMEM = pl.BlockSpec(memory_space=pltpu.SMEM)
HBM = pl.BlockSpec(memory_space=pl.ANY)


def call(kernel, name, where, outs, scratch):
    return pl.pallas_call(
        kernel,
        name=name,
        in_specs=where,
        out_specs=[VMEM] * len(outs),
        out_shape=[jax.ShapeDtypeStruct(s, d) for s, d in outs],
        scratch_shapes=scratch,
    )


def dma(n):
    return pltpu.SemaphoreType.DMA((n,))


def reduce_rows(packed, slabs):
    rest = slabs // 4
    me = lax.axis_index("slab")
    core, side, far = me % 2, (me // 2) % 2, me // 4
    half = packed.reshape(2, 2 * rest, *packed.shape[1:])

    def take(x, i):
        return lax.dynamic_index_in_dim(x, i, 0, keepdims=False)

    def swap(x, bit):
        return lax.ppermute(x, "slab", [(i, i ^ bit) for i in range(slabs)])

    mine = (take(half, core).astype(F32) + swap(take(half, 1 - core), 1).astype(F32)).astype(BF16)
    half = mine.reshape(2, rest, *packed.shape[1:])
    mine = (take(half, side).astype(F32) + swap(take(half, 1 - side), 2).astype(F32)).astype(BF16)
    total = take(mine, far).astype(F32)
    for d in range(1, rest):
        total = total + swap(take(mine, far ^ d), 4 * d).astype(F32)
    return total


def body(latents, positions, counts, send_rows, tiles, w_msg, w_in, w_out, cotangent):
    n, width = latents.shape
    hidden_width = w_out.shape[1]
    slabs = lax.axis_size("slab")
    norm = 1.0 / math.sqrt(slabs * n)
    rows = send_rows[0]
    near = tiles[0]
    up_pairs = [(i, i + 1) for i in range(slabs - 1)]
    down_pairs = [(i + 1, i) for i in range(slabs - 1)]

    def go_up(x):
        return lax.ppermute(x, "slab", up_pairs)

    def go_down(x):
        return lax.ppermute(x, "slab", down_pairs)

    row_b, row_f = ((n, width), BF16), ((n, width), F32)
    hid_b = ((n, hidden_width), BF16)
    halo_b = ((HALO, width), BF16)
    square = pltpu.VMEM((width, width), BF16)
    w_in_buf = pltpu.VMEM((width, hidden_width), BF16)
    w_out_buf = pltpu.VMEM((hidden_width, width), BF16)

    up, down = call(
        send_kernel, "send", [SMEM, VMEM, VMEM, VMEM],
        [((HALO + GEO, width), BF16)] * 2, [pltpu.VMEM((GEO, n), F32)],
    )(counts, rows, latents, positions)
    lower, upper = go_up(up), go_down(down)

    a_own, squares, columns, update, partial, pre_part, grad_hidden = call(
        own_kernel, "own", [SMEM, SMEM, VMEM, VMEM, VMEM, HBM, HBM, HBM],
        [((n, n), BF16), ((n, TILE), F32), ((n, TILE), F32), row_b, row_f, hid_b, hid_b],
        [square, w_in_buf, w_out_buf, pltpu.VMEM((TILE, n), F32), pltpu.VMEM((n // TILE, 8, TILE), F32), dma(3)],
    )(counts, near, latents, positions, cotangent, w_msg, w_in, w_out)

    a_ghost, inverse, message0, hidden0, slope0, current1, update1, up, down = call(
        first_kernel, "first", [SMEM, SMEM] + [VMEM] * 8 + [HBM] * 3,
        [((n, 2 * HALO), BF16), ((n, TILE), F32), row_b, hid_b, hid_b, row_b, row_b, halo_b, halo_b],
        [square, w_in_buf, w_out_buf, square, pltpu.VMEM((2 * GHOST_TILES, 8, TILE), F32),
         pltpu.VMEM((n, TILE), F32), dma(4)],
    )(counts, near, rows, latents, lower, upper, squares, columns, partial, pre_part, w_msg, w_in, w_out)
    lower, upper = go_up(up), go_down(down)

    partial, pre_part = call(
        middle_kernel, "middle", [VMEM] * 3 + [HBM], [row_f, hid_b], [w_in_buf, dma(1)],
    )(current1, update1, a_own, w_in)

    message1, hidden1, grad_pre1, scaled1, back_lower, back_upper = call(
        last_kernel, "last", [VMEM] * 7 + [HBM], [row_b, hid_b, hid_b, row_b, halo_b, halo_b],
        [w_in_buf, dma(1)],
    )(lower, upper, a_ghost, inverse, partial, pre_part, grad_hidden, w_in)
    from_above, from_below = go_down(back_lower), go_up(back_upper)

    out_rows, msg_rows = hidden_width // slabs, width // slabs
    in_rows = 2 * msg_rows * (hidden_width // width)
    grad_own, direct, packed, final = call(
        functools.partial(terms_kernel, True, slabs, norm), "terms1", [SMEM] + [VMEM] * 7 + [HBM] * 2,
        [row_f, row_f, ((slabs, out_rows + in_rows, width), BF16), row_b],
        [w_in_buf, w_out_buf, pltpu.VMEM((8, TILE), F32), dma(2)],
    )(counts, current1, message1, hidden1, grad_pre1, scaled1, cotangent, a_own, w_in, w_out)
    share1 = reduce_rows(packed, slabs)

    grad_update1, gradient1, grad_pre0, scaled0, back_lower, back_upper = call(
        turn_kernel, "turn", [SMEM] + [VMEM] * 8 + [HBM] * 3,
        [row_b, row_f, hid_b, row_b, halo_b, halo_b],
        [square, w_in_buf, w_out_buf, dma(3)],
    )(counts, rows, grad_own, from_above, from_below, direct, slope0, inverse, a_ghost, w_msg, w_in, w_out)
    from_above, from_below = go_down(back_lower), go_up(back_upper)

    grad_own, direct, packed = call(
        functools.partial(terms_kernel, False, slabs, norm), "terms0", [SMEM] + [VMEM] * 9 + [HBM],
        [row_f, row_f, ((slabs, msg_rows + out_rows + in_rows, width), BF16)],
        [w_in_buf, pltpu.VMEM((8, TILE), F32), dma(1)],
    )(counts, latents, message0, hidden0, grad_pre0, scaled0, gradient1, current1, grad_update1, a_own, w_in)
    share0 = reduce_rows(packed, slabs)

    gradient, packed = call(
        functools.partial(end_kernel, slabs, norm), "end", [VMEM] * 6 + [HBM],
        [row_f, ((slabs, msg_rows, width), BF16)],
        [square, pltpu.VMEM((n, width), BF16), dma(1)],
    )(rows, grad_own, from_above, from_below, direct, latents, w_msg)
    share_msg0 = reduce_rows(packed, slabs)

    def unpack_in(share):
        parts = share.reshape(2, hidden_width // width, msg_rows, width)
        return jnp.concatenate([parts[:, h] for h in range(hidden_width // width)], axis=-1)

    grad_msg = jnp.stack([share_msg0, share0[:msg_rows]])
    grad_out = jnp.stack([share0[msg_rows : msg_rows + out_rows], share1[:out_rows]])
    grad_in = jnp.stack([unpack_in(share0[msg_rows + out_rows :]), unpack_in(share1[out_rows:])])
    return (final, gradient, grad_msg, grad_in, grad_out)


def solution(mesh):
    placed = (
        P(("groups", "slab"), None),
        P(None, ("groups", "slab")),
        P(("groups", "slab")),
        P(("groups", "slab"), None, None),
        P(("groups", "slab"), None, None),
        P(),
        P(),
        P(),
        P(("groups", "slab"), None),
    )
    return jax.shard_map(
        body,
        mesh=mesh,
        in_specs=placed,
        out_specs=(
            P(("groups", "slab"), None),
            P(("groups", "slab"), None),
            P("groups", "slab", None),
            P("groups", None, "slab", None),
            P("groups", "slab", None),
        ),
        check_vma=False,
    )
```

```python
import functools
import math

import jax
import jax.numpy as jnp
from jax import lax
from jax.experimental import pallas as pl
from jax.experimental.pallas import tpu as pltpu
from jax.sharding import PartitionSpec as P


LAYERS = 2
TILE = 128
HALO = 256
GEO = 16
BLOCK = 256
LIMIT = 24
GHOST_TILES = HALO // TILE
F32 = jnp.float32
BF16 = jnp.bfloat16


def dg(a, b, ca, cb):
    return lax.dot_general(a, b, (((ca,), (cb,)), ((), ())), preferred_element_type=F32)


def blocks(n):
    return [slice(r, r + BLOCK) for r in range(0, n, BLOCK)]


def alive_rows(count_ref, rows, start=0):
    index = lax.broadcasted_iota(jnp.int32, (rows, 1), 0) + start
    return jnp.where(index < count_ref[0], 1.0, 0.0).astype(F32)


def picks(rows_ref, d, n):
    index = lax.broadcasted_iota(jnp.int32, (n, HALO), 0)
    return jnp.where(index == rows_ref[d : d + 1, :], 1.0, 0.0).astype(BF16)


def send_kernel(count, rows, latents, positions, up, down, geo):
    n = latents.shape[0]
    x = positions[...]
    high = x.astype(BF16).astype(F32)
    rest = x - high
    middle = rest.astype(BF16).astype(F32)
    geo[...] = jnp.zeros_like(geo)
    geo[0:3, :] = high
    geo[3:6, :] = middle
    geo[6:9, :] = rest - middle
    lane = lax.broadcasted_iota(jnp.int32, (1, n), 1)
    geo[9:10, :] = jnp.where(lane < count[0], 1.0, 0.0).astype(F32)
    fields = geo[...].astype(BF16)
    for d, out in ((0, down), (1, up)):
        pick = picks(rows, d, n)
        out[0:HALO, :] = dg(pick, latents[...], 0, 0).astype(BF16)
        out[HALO : HALO + GEO, :] = jnp.zeros((GEO, out.shape[1]), BF16)
        out[HALO : HALO + GEO, 0:HALO] = dg(fields, pick, 1, 0).astype(BF16)


def pair_weight(x_column, geo):
    total = None
    for c in range(3):
        offset = x_column[:, c : c + 1] - geo[c : c + 1, :]
        total = offset * offset if total is None else total + offset * offset
    return geo[3:4, :] / (1.0 + total)


def own_kernel(
    count, tiles, latents, positions, cotangent, w_msg, w_in, w_out,
    a_own, squares, columns, update, partial, pre_part, grad_hidden,
    wide, geo,
):
    n = latents.shape[0]
    tile_count = n // TILE
    wide[...] = jnp.zeros_like(wide)
    wide[0:3, :] = positions[...]
    lane = lax.broadcasted_iota(jnp.int32, (1, n), 1)
    wide[3:4, :] = jnp.where(lane < count[0], 1.0, 0.0).astype(F32)
    for t in range(tile_count):
        part = wide[:, t * TILE : (t + 1) * TILE]
        geo[t] = part[0:8]
        columns[t * TILE : (t + 1) * TILE, :] = part.T
    a_own[...] = jnp.zeros_like(a_own)
    squares[...] = jnp.zeros_like(squares)

    def tile_step(t, _):
        rows = pl.ds(pl.multiple_of(t * TILE, TILE), TILE)
        for k in range(tiles.shape[2]):
            near = tiles[0, t, k] - GHOST_TILES

            @pl.when((near >= 0) & (near < tile_count))
            def _():
                weight = pair_weight(columns[rows, :], geo[near])
                squares[rows, :] += weight * weight
                a_own[rows, pl.ds(pl.multiple_of(near * TILE, TILE), TILE)] = weight.astype(BF16)

        return 0

    lax.fori_loop(0, tile_count, tile_step, 0)
    update[...] = dg(latents[...], w_msg[0], 1, 0).astype(BF16)
    partial[...] = dg(a_own[...], update[...], 1, 0)
    pre_part[...] = dg(latents[...], w_in[0, 0], 1, 0).astype(BF16)
    grad_delta = (cotangent[...].astype(F32) * alive_rows(count, n)).astype(BF16)
    grad_hidden[...] = dg(grad_delta, w_out[LAYERS - 1], 1, 1).astype(BF16)


def first_kernel(
    count, tiles, rows, latents, lower, upper, squares, columns, partial, pre_part, w_msg, w_in, w_out,
    a_ghost, inverse, message, hidden, slope, current, update, up, down,
    geo, sums,
):
    n = latents.shape[0]
    tile_count = n // TILE
    for side, ghost in enumerate((lower, upper)):
        fields = ghost[HALO : HALO + GEO, :].astype(F32)
        place = fields[0:3] + fields[3:6] + fields[6:9]
        for g in range(GHOST_TILES):
            cut = slice(g * TILE, (g + 1) * TILE)
            geo[side * GHOST_TILES + g, 0:3, :] = place[:, cut]
            geo[side * GHOST_TILES + g, 3:4, :] = fields[9:10, cut]
    a_ghost[...] = jnp.zeros_like(a_ghost)
    sums[...] = squares[...]

    def tile_step(t, _):
        own = pl.ds(pl.multiple_of(t * TILE, TILE), TILE)
        for k in range(tiles.shape[2]):
            index = tiles[0, t, k]
            near = jnp.where(index < GHOST_TILES, index, index - tile_count)

            @pl.when((index < GHOST_TILES) | (index >= GHOST_TILES + tile_count))
            def _():
                weight = pair_weight(columns[own, :], geo[near])
                sums[own, :] += weight * weight
                a_ghost[own, pl.ds(pl.multiple_of(near * TILE, TILE), TILE)] = weight.astype(BF16)

        return 0

    lax.fori_loop(0, tile_count, tile_step, 0)
    update_lower = dg(lower[0:HALO, :], w_msg[0], 1, 0).astype(BF16)
    update_upper = dg(upper[0:HALO, :], w_msg[0], 1, 0).astype(BF16)
    for r in blocks(n):
        inv = 1.0 / jnp.sqrt(1.0 + jnp.sum(sums[r, :], axis=1, keepdims=True))
        inverse[r, :] = jnp.broadcast_to(inv, (BLOCK, TILE))
        total = partial[r, :] + dg(a_ghost[r, 0:HALO], update_lower, 1, 0)
        total = total + dg(a_ghost[r, HALO : 2 * HALO], update_upper, 1, 0)
        mess = (total * inv).astype(BF16)
        message[r, :] = mess
        pre = pre_part[r, :].astype(F32) + dg(mess, w_in[0, 1], 1, 0)
        sigma = 1.0 / (1.0 + jnp.exp(-pre))
        hid = (pre * sigma).astype(BF16)
        hidden[r, :] = hid
        slope[r, :] = (sigma * (1.0 + pre * (1.0 - sigma))).astype(BF16)
        delta = dg(hid, w_out[0], 1, 0)
        live = alive_rows(count, BLOCK, r.start)
        cur = (latents[r, :].astype(F32) + live * delta).astype(BF16)
        current[r, :] = cur
        update[r, :] = dg(cur, w_msg[1], 1, 0).astype(BF16)
    down[...] = dg(picks(rows, 0, n), update[...], 0, 0).astype(BF16)
    up[...] = dg(picks(rows, 1, n), update[...], 0, 0).astype(BF16)


def middle_kernel(current, update, a_own, w_in, partial, pre_part):
    partial[...] = dg(a_own[...], update[...], 1, 0)
    pre_part[...] = dg(current[...], w_in[1, 0], 1, 0).astype(BF16)


def last_kernel(
    lower, upper, a_ghost, inverse, partial, pre_part, grad_hidden, w_in,
    message, hidden, grad_pre, scaled, back_lower, back_upper,
):
    n = partial.shape[0]
    for r in blocks(n):
        inv = inverse[r, 0:1]
        total = partial[r, :] + dg(a_ghost[r, 0:HALO], lower[...], 1, 0)
        total = total + dg(a_ghost[r, HALO : 2 * HALO], upper[...], 1, 0)
        mess = (total * inv).astype(BF16)
        message[r, :] = mess
        pre = pre_part[r, :].astype(F32) + dg(mess, w_in[1, 1], 1, 0)
        sigma = 1.0 / (1.0 + jnp.exp(-pre))
        hidden[r, :] = (pre * sigma).astype(BF16)
        slope = sigma * (1.0 + pre * (1.0 - sigma))
        gpre = (grad_hidden[r, :].astype(F32) * slope).astype(BF16)
        grad_pre[r, :] = gpre
        scaled[r, :] = (dg(gpre, w_in[1, 1], 1, 1) * inv).astype(BF16)
    back_lower[...] = dg(a_ghost[:, 0:HALO], scaled[...], 0, 0).astype(BF16)
    back_upper[...] = dg(a_ghost[:, HALO : 2 * HALO], scaled[...], 0, 0).astype(BF16)


def pack_rows(core, stage, value, keep, give, at, slabs):
    height, columns = value.shape
    rows, width, rest = height // slabs, keep.shape[-1], slabs // 4
    stage[0:height, 0:columns] = value
    for h in range(columns // width):
        for side in range(2):
            for far in range(rest):
                pair = (far * 2 + side) * 2
                for out, which in ((keep, core), (give, 1 - core)):
                    source = pl.ds(pl.multiple_of((pair + which) * rows, rows), rows)
                    out[side * rest + far, at : at + rows, :] = stage[source, h * width : (h + 1) * width]
        at += rows
    return at


def terms_kernel(layer, slabs, norm, *refs):
    if layer == 1:
        (count, core, before, message, hidden, grad_pre, scaled, vector, a_own, w_in, w_out,
         grad_own, direct, keep, give, final, stage, tall) = refs
    else:
        (count, core, before, message, hidden, grad_pre, scaled, vector, later, later_update, a_own, w_in,
         grad_own, direct, keep, give, stage, tall) = refs
    n = before.shape[0]
    live = alive_rows(count, n)
    grad_delta = (vector[...].astype(F32) * live).astype(BF16)
    at = 0
    if layer == 0:
        value = dg(later[...], later_update[...], 0, 0)
        at = pack_rows(core[0], tall, (value * norm).astype(BF16), keep, give, at, slabs)
    value = dg(hidden[...], grad_delta, 0, 0)
    at = pack_rows(core[0], tall, (value * norm).astype(BF16), keep, give, at, slabs)
    for left in (before, message):
        value = dg(left[...], grad_pre[...], 0, 0)
        at = pack_rows(core[0], stage, (value * norm).astype(BF16), keep, give, at, slabs)
    grad_own[...] = dg(a_own[...], scaled[...], 0, 0)
    direct[...] = vector[...].astype(F32) + dg(grad_pre[...], w_in[layer, 0], 1, 1)
    if layer == 1:
        delta = dg(hidden[...], w_out[layer], 1, 0)
        final[...] = (before[...].astype(F32) + live * delta).astype(BF16)


def turn_kernel(
    count, rows, grad_own, from_above, from_below, direct, slope, inverse, a_ghost, w_msg, w_in, w_out,
    grad_update, gradient, grad_pre, scaled, back_lower, back_upper,
):
    n = direct.shape[0]
    pick_down = picks(rows, 0, n)
    pick_up = picks(rows, 1, n)
    for r in blocks(n):
        total = grad_own[r, :] + dg(pick_up[r, :], from_above[...], 1, 0)
        total = total + dg(pick_down[r, :], from_below[...], 1, 0)
        gup = total.astype(BF16)
        grad_update[r, :] = gup
        grad = direct[r, :] + dg(gup, w_msg[1], 1, 1)
        gradient[r, :] = grad
        gdelta = (grad * alive_rows(count, BLOCK, r.start)).astype(BF16)
        gpre = (dg(gdelta, w_out[0], 1, 1) * slope[r, :].astype(F32)).astype(BF16)
        grad_pre[r, :] = gpre
        scaled[r, :] = (dg(gpre, w_in[0, 1], 1, 1) * inverse[r, 0:1]).astype(BF16)
    back_lower[...] = dg(a_ghost[:, 0:HALO], scaled[...], 0, 0).astype(BF16)
    back_upper[...] = dg(a_ghost[:, HALO : 2 * HALO], scaled[...], 0, 0).astype(BF16)


def end_kernel(
    slabs, norm, core, rows, grad_own, from_above, from_below, direct, latents, w_msg,
    gradient, keep, give, gup_all, tall,
):
    n = direct.shape[0]
    pick_down = picks(rows, 0, n)
    pick_up = picks(rows, 1, n)
    total = grad_own[...] + dg(pick_up, from_above[...], 1, 0)
    total = total + dg(pick_down, from_below[...], 1, 0)
    gup_all[...] = total.astype(BF16)
    value = dg(latents[...], gup_all[...], 0, 0)
    pack_rows(core[0], tall, (value * norm).astype(BF16), keep, give, 0, slabs)
    gradient[...] = direct[...] + dg(gup_all[...], w_msg[0], 1, 1)


VMEM = pl.BlockSpec(memory_space=pltpu.VMEM)
SMEM = pl.BlockSpec(memory_space=pltpu.SMEM)


def call(kernel, where, outs, scratch, gflops):
    def run(*args):
        return pl.pallas_call(
            kernel,
            in_specs=where,
            out_specs=[VMEM] * len(outs),
            out_shape=[jax.ShapeDtypeStruct(s, d) for s, d in outs],
            scratch_shapes=scratch,
            compiler_params=pltpu.CompilerParams(vmem_limit_bytes=LIMIT << 20),
            cost_estimate=pl.CostEstimate(flops=int(gflops * 1e9), transcendentals=0, bytes_accessed=int(gflops * 2e6)),
        )(*args)

    return run


def reduce_rows(keep, give, slabs):
    rest = slabs // 4
    me = lax.axis_index("slab")
    side, far = (me // 2) % 2, me // 4

    def take(x, i):
        return lax.dynamic_index_in_dim(x, i, 0, keepdims=False)

    def swap(x, bit):
        return lax.ppermute(x, "slab", [(i, i ^ bit) for i in range(slabs)])

    mine = (keep.astype(F32) + swap(give, 1).astype(F32)).astype(BF16)
    half = mine.reshape(2, rest, *keep.shape[1:])
    mine = (take(half, side).astype(F32) + swap(take(half, 1 - side), 2).astype(F32)).astype(BF16)
    total = take(mine, far).astype(F32)
    for d in range(1, rest):
        total = total + swap(take(mine, far ^ d), 4 * d).astype(F32)
    return total


def body(latents, positions, counts, send_rows, tiles, w_msg, w_in, w_out, cotangent):
    n, width = latents.shape
    hidden_width = w_out.shape[1]
    slabs = lax.axis_size("slab")
    norm = 1.0 / math.sqrt(slabs * n)
    rows = send_rows[0]
    core = (lax.axis_index("slab") % 2).astype(jnp.int32).reshape(1)
    up_pairs = [(i, i + 1) for i in range(slabs - 1)]
    down_pairs = [(i + 1, i) for i in range(slabs - 1)]

    def trade(up, down):
        lower = lax.ppermute(up, "slab", up_pairs)
        upper = lax.ppermute(down, "slab", down_pairs)
        return lower, upper

    row_b, row_f = ((n, width), BF16), ((n, width), F32)
    hid_b = ((n, hidden_width), BF16)
    halo_b = ((HALO, width), BF16)
    stage = pltpu.VMEM((width, hidden_width), BF16)
    tall = pltpu.VMEM((hidden_width, width), BF16)

    up, down = call(
        send_kernel, [SMEM, VMEM, VMEM, VMEM],
        [((HALO + GEO, width), BF16)] * 2, [pltpu.VMEM((GEO, n), F32)], 0.5,
    )(counts, rows, latents, positions)
    lower, upper = trade(up, down)

    a_own, squares, columns, _, partial, pre_part, grad_hidden = call(
        own_kernel, [SMEM, SMEM] + [VMEM] * 6,
        [((n, n), BF16), ((n, TILE), F32), ((n, TILE), F32), row_b, row_f, hid_b, hid_b],
        [pltpu.VMEM((TILE, n), F32), pltpu.VMEM((n // TILE, 8, TILE), F32)], 5,
    )(counts, tiles, latents, positions, cotangent, w_msg, w_in, w_out)

    a_ghost, inverse, message0, hidden0, slope0, current1, update1, up, down = call(
        first_kernel, [SMEM, SMEM] + [VMEM] * 11,
        [((n, 2 * HALO), BF16), ((n, TILE), F32), row_b, hid_b, hid_b, row_b, row_b, halo_b, halo_b],
        [pltpu.VMEM((2 * GHOST_TILES, 8, TILE), F32), pltpu.VMEM((n, TILE), F32)], 5,
    )(counts, tiles, rows, latents, lower, upper, squares, columns, partial, pre_part, w_msg, w_in, w_out)
    lower, upper = trade(up, down)

    partial, pre_part = call(middle_kernel, [VMEM] * 4, [row_f, hid_b], [], 2)(current1, update1, a_own, w_in)

    message1, hidden1, grad_pre1, scaled1, back_lower, back_upper = call(
        last_kernel, [VMEM] * 8, [row_b, hid_b, hid_b, row_b, halo_b, halo_b], [], 4,
    )(lower, upper, a_ghost, inverse, partial, pre_part, grad_hidden, w_in)
    from_below, from_above = trade(back_upper, back_lower)

    out_rows, msg_rows = hidden_width // slabs, width // slabs
    in_rows = 2 * msg_rows * (hidden_width // width)
    half = ((slabs // 2, out_rows + in_rows, width), BF16)
    grad_own, direct, keep, give, final = call(
        functools.partial(terms_kernel, 1, slabs, norm), [SMEM] * 2 + [VMEM] * 9,
        [row_f, row_f, half, half, row_b], [stage, tall], 6,
    )(counts, core, current1, message1, hidden1, grad_pre1, scaled1, cotangent, a_own, w_in, w_out)
    share1 = reduce_rows(keep, give, slabs)

    grad_update1, gradient1, grad_pre0, scaled0, back_lower, back_upper = call(
        turn_kernel, [SMEM] + [VMEM] * 11, [row_b, row_f, hid_b, row_b, halo_b, halo_b], [], 4,
    )(counts, rows, grad_own, from_above, from_below, direct, slope0, inverse, a_ghost, w_msg, w_in, w_out)
    from_below, from_above = trade(back_upper, back_lower)

    half = ((slabs // 2, msg_rows + out_rows + in_rows, width), BF16)
    grad_own, direct, keep, give = call(
        functools.partial(terms_kernel, 0, slabs, norm), [SMEM] * 2 + [VMEM] * 10,
        [row_f, row_f, half, half], [stage, tall], 6,
    )(counts, core, latents, message0, hidden0, grad_pre0, scaled0, gradient1, current1, grad_update1, a_own, w_in)
    share0 = reduce_rows(keep, give, slabs)

    half = ((slabs // 2, msg_rows, width), BF16)
    gradient, keep, give = call(
        functools.partial(end_kernel, slabs, norm), [SMEM] + [VMEM] * 7, [row_f, half, half],
        [pltpu.VMEM((n, width), BF16), tall], 2,
    )(core, rows, grad_own, from_above, from_below, direct, latents, w_msg)
    share_msg0 = reduce_rows(keep, give, slabs)

    def unpack_in(share):
        parts = share.reshape(2, hidden_width // width, msg_rows, width)
        return jnp.concatenate([parts[:, h] for h in range(hidden_width // width)], axis=-1)

    grad_msg = jnp.stack([share_msg0, share0[:msg_rows]])
    grad_out = jnp.stack([share0[msg_rows : msg_rows + out_rows], share1[:out_rows]])
    grad_in = jnp.stack([unpack_in(share0[msg_rows + out_rows :]), unpack_in(share1[out_rows:])])
    return (final, gradient, grad_msg, grad_in, grad_out)


def solution(mesh):
    placed = (
        P(("groups", "slab"), None),
        P(None, ("groups", "slab")),
        P(("groups", "slab")),
        P(("groups", "slab"), None, None),
        P(("groups", "slab"), None, None),
        P(),
        P(),
        P(),
        P(("groups", "slab"), None),
    )
    return jax.shard_map(
        body,
        mesh=mesh,
        in_specs=placed,
        out_specs=(
            P(("groups", "slab"), None),
            P(("groups", "slab"), None),
            P("groups", "slab", None),
            P("groups", None, "slab", None),
            P("groups", "slab", None),
        ),
        check_vma=False,
    )
```

```python
import functools
import math

import jax
import jax.numpy as jnp
from jax import lax
from jax.experimental import pallas as pl
from jax.experimental.pallas import tpu as pltpu
from jax.sharding import PartitionSpec as P


TILE = 128
HALO = 256
GEO = 16
BLOCK = 256
LIMIT = 16
WHOLE = 50
GHOST_TILES = HALO // TILE
F32 = jnp.float32
BF16 = jnp.bfloat16


def dg(a, b, ca, cb):
    return lax.dot_general(a, b, (((ca,), (cb,)), ((), ())), preferred_element_type=F32)


def blocks(n):
    return [slice(r, r + BLOCK) for r in range(0, n, BLOCK)]


def alive_rows(count, rows, start=0):
    index = lax.broadcasted_iota(jnp.int32, (rows, 1), 0) + start
    return jnp.where(index < count[0], 1.0, 0.0).astype(F32)


def picks(rows, d, n):
    index = lax.broadcasted_iota(jnp.int32, (n, HALO), 0)
    return jnp.where(index == rows[pl.ds(d, 1), :], 1.0, 0.0).astype(BF16)


def send_kernel(scalars, count, core, rows, latents_far, positions_far, w_msg, w_in, *refs):
    near, far, latents, positions, wm, wi, geo, sems = refs[scalars:]
    n = latents.shape[0]
    moves = ((positions_far, positions), (latents_far, latents), (w_msg.at[0], wm), (w_in.at[0, 0], wi))
    copies = [pltpu.make_async_copy(src, dst, sems.at[i]) for i, (src, dst) in enumerate(moves)]
    for copy in copies:
        copy.start()
    copies[0].wait()
    x = positions[...]
    high = x.astype(BF16).astype(F32)
    rest = x - high
    middle = rest.astype(BF16).astype(F32)
    geo[...] = jnp.zeros_like(geo)
    geo[0:3, :] = high
    geo[3:6, :] = middle
    geo[6:9, :] = rest - middle
    lane = lax.broadcasted_iota(jnp.int32, (1, n), 1)
    geo[9:10, :] = jnp.where(lane < count[0], 1.0, 0.0).astype(F32)
    fields = geo[...].astype(BF16)
    copies[1].wait()
    for d, out in ((1 - core[0], near), (core[0], far)):
        pick = picks(rows, d, n)
        out[0:HALO, :] = dg(pick, latents[...], 0, 0).astype(BF16)
        out[HALO : HALO + GEO, :] = jnp.zeros((GEO, out.shape[1]), BF16)
        out[HALO : HALO + GEO, 0:HALO] = dg(fields, pick, 1, 0).astype(BF16)
    copies[2].wait()
    copies[3].wait()


def pair_weight(x_column, geo):
    total = None
    for c in range(3):
        offset = x_column[:, c : c + 1] - geo[c : c + 1, :]
        total = offset * offset if total is None else total + offset * offset
    return geo[3:4, :] / (1.0 + total)


def own_kernel(
    count, tiles, latents, positions, wm, wi,
    a_own, squares, columns, update, partial, pre_part,
    wide, geo,
):
    n = latents.shape[0]
    tile_count = n // TILE
    wide[...] = jnp.zeros_like(wide)
    wide[0:3, :] = positions[...]
    lane = lax.broadcasted_iota(jnp.int32, (1, n), 1)
    wide[3:4, :] = jnp.where(lane < count[0], 1.0, 0.0).astype(F32)
    for t in range(tile_count):
        part = wide[:, t * TILE : (t + 1) * TILE]
        geo[t] = part[0:8]
        columns[t * TILE : (t + 1) * TILE, :] = part.T
    a_own[...] = jnp.zeros_like(a_own)
    squares[...] = jnp.zeros_like(squares)

    def tile_step(t, _):
        rows = pl.ds(pl.multiple_of(t * TILE, TILE), TILE)
        for k in range(tiles.shape[2]):
            tile = tiles[0, t, k] - GHOST_TILES

            @pl.when((tile >= 0) & (tile < tile_count))
            def _():
                weight = pair_weight(columns[rows, :], geo[tile])
                squares[rows, :] += weight * weight
                a_own[rows, pl.ds(pl.multiple_of(tile * TILE, TILE), TILE)] = weight.astype(BF16)

        return 0

    lax.fori_loop(0, tile_count, tile_step, 0)
    update[...] = dg(latents[...], wm[...], 1, 0).astype(BF16)
    partial[...] = dg(a_own[...], update[...], 1, 0)
    pre_part[...] = dg(latents[...], wi[...], 1, 0).astype(BF16)


def first_kernel(
    count, core, tiles, rows, latents, near, far, squares, columns, partial, pre_part, wm, w_in, w_out, w_msg,
    a_ghost, inverse, message, hidden, slope, current, update, send_near, send_far,
    geo, sums,
):
    n = latents.shape[0]
    tile_count = n // TILE
    for side, ghost in enumerate((near, far)):
        fields = ghost[HALO : HALO + GEO, :].astype(F32)
        place = fields[0:3] + fields[3:6] + fields[6:9]
        for g in range(GHOST_TILES):
            cut = slice(g * TILE, (g + 1) * TILE)
            geo[side * GHOST_TILES + g, 0:3, :] = place[:, cut]
            geo[side * GHOST_TILES + g, 3:4, :] = fields[9:10, cut]
    a_ghost[...] = jnp.zeros_like(a_ghost)
    sums[...] = squares[...]
    below = GHOST_TILES * (1 - core[0])
    above = GHOST_TILES * core[0] - (GHOST_TILES + tile_count)

    def tile_step(t, _):
        own = pl.ds(pl.multiple_of(t * TILE, TILE), TILE)
        for k in range(tiles.shape[2]):
            index = tiles[0, t, k]
            tile = jnp.where(index < GHOST_TILES, index + below, index + above)

            @pl.when((index < GHOST_TILES) | (index >= GHOST_TILES + tile_count))
            def _():
                weight = pair_weight(columns[own, :], geo[tile])
                sums[own, :] += weight * weight
                a_ghost[own, pl.ds(pl.multiple_of(tile * TILE, TILE), TILE)] = weight.astype(BF16)

        return 0

    lax.fori_loop(0, tile_count, tile_step, 0)
    update_near = dg(near[0:HALO, :], wm[...], 1, 0).astype(BF16)
    update_far = dg(far[0:HALO, :], wm[...], 1, 0).astype(BF16)
    for r in blocks(n):
        inv = 1.0 / jnp.sqrt(1.0 + jnp.sum(sums[r, :], axis=1, keepdims=True))
        inverse[r, :] = jnp.broadcast_to(inv, (BLOCK, TILE))
        total = partial[r, :] + dg(a_ghost[r, 0:HALO], update_near, 1, 0)
        total = total + dg(a_ghost[r, HALO : 2 * HALO], update_far, 1, 0)
        mess = (total * inv).astype(BF16)
        message[r, :] = mess
        pre = pre_part[r, :].astype(F32) + dg(mess, w_in[0, 1], 1, 0)
        sigma = 1.0 / (1.0 + jnp.exp(-pre))
        hid = (pre * sigma).astype(BF16)
        hidden[r, :] = hid
        slope[r, :] = (sigma * (1.0 + pre * (1.0 - sigma))).astype(BF16)
        delta = dg(hid, w_out[0], 1, 0)
        live = alive_rows(count, BLOCK, r.start)
        cur = (latents[r, :].astype(F32) + live * delta).astype(BF16)
        current[r, :] = cur
        update[r, :] = dg(cur, w_msg[1], 1, 0).astype(BF16)
    send_near[...] = dg(picks(rows, 1 - core[0], n), update[...], 0, 0).astype(BF16)
    send_far[...] = dg(picks(rows, core[0], n), update[...], 0, 0).astype(BF16)


def middle_kernel(
    count, current, update, a_own, cot, w_in, w_out,
    partial, pre_part, grad_delta, grad_hidden,
):
    n = current.shape[0]
    partial[...] = dg(a_own[...], update[...], 1, 0)
    pre_part[...] = dg(current[...], w_in[1, 0], 1, 0).astype(BF16)
    grad_delta[...] = (cot[...].astype(F32) * alive_rows(count, n)).astype(BF16)
    grad_hidden[...] = dg(grad_delta[...], w_out[1], 1, 1).astype(BF16)


def last_kernel(
    near, far, a_ghost, inverse, partial, pre_part, grad_hidden, w_in,
    message, hidden, grad_pre, scaled, back_near, back_far,
):
    n = partial.shape[0]
    for r in blocks(n):
        inv = inverse[r, 0:1]
        total = partial[r, :] + dg(a_ghost[r, 0:HALO], near[...], 1, 0)
        total = total + dg(a_ghost[r, HALO : 2 * HALO], far[...], 1, 0)
        mess = (total * inv).astype(BF16)
        message[r, :] = mess
        pre = pre_part[r, :].astype(F32) + dg(mess, w_in[1, 1], 1, 0)
        sigma = 1.0 / (1.0 + jnp.exp(-pre))
        hidden[r, :] = (pre * sigma).astype(BF16)
        slope = sigma * (1.0 + pre * (1.0 - sigma))
        gpre = (grad_hidden[r, :].astype(F32) * slope).astype(BF16)
        grad_pre[r, :] = gpre
        scaled[r, :] = (dg(gpre, w_in[1, 1], 1, 1) * inv).astype(BF16)
    back_near[...] = dg(a_ghost[:, 0:HALO], scaled[...], 0, 0).astype(BF16)
    back_far[...] = dg(a_ghost[:, HALO : 2 * HALO], scaled[...], 0, 0).astype(BF16)


def pack_rows(core, stage, value, keep, give, at, slabs):
    height, columns = value.shape
    rows, width, bits = height // slabs, keep.shape[-1], slabs.bit_length() - 2
    stage[0:height, 0:columns] = value
    for h in range(columns // width):
        for pair in range(slabs // 2):
            place = sum(((pair >> b) & 1) << (bits - 1 - b) for b in range(bits))
            for out, which in ((keep, core), (give, 1 - core)):
                source = pl.ds(pl.multiple_of((pair * 2 + which) * rows, rows), rows)
                out[place, at : at + rows, :] = stage[source, h * width : (h + 1) * width]
        at += rows
    return at


def terms_kernel(plan, slabs, norm, core, *refs):
    wide, tall = refs[-2:]
    outs = refs[len(refs) - 2 - 2 * len(plan) : -2]
    for c, chunk in enumerate(plan):
        at = 0
        for a, b in chunk:
            value = (dg(refs[a][...], refs[b][...], 0, 0) * norm).astype(BF16)
            stage = tall if value.shape[1] == tall.shape[1] else wide
            at = pack_rows(core[0], stage, value, outs[2 * c], outs[2 * c + 1], at, slabs)


def flow1_kernel(
    count, before, hidden, grad_pre, scaled, a_own, cot, w_in, w_out,
    grad_own, direct, final,
):
    grad_own[...] = dg(a_own[...], scaled[...], 0, 0)
    direct[...] = cot[...].astype(F32) + dg(grad_pre[...], w_in[1, 0], 1, 1)
    delta = dg(hidden[...], w_out[1], 1, 0)
    live = alive_rows(count, before.shape[0])
    final[...] = (before[...].astype(F32) + live * delta).astype(BF16)


def flow0_kernel(gradient, grad_pre, scaled, a_own, w_in, grad_own, direct):
    grad_own[...] = dg(a_own[...], scaled[...], 0, 0)
    direct[...] = gradient[...] + dg(grad_pre[...], w_in[0, 0], 1, 1)


def turn_kernel(
    count, core, rows, grad_own, near, far, direct, slope, inverse, a_ghost, w_msg, w_in, w_out,
    grad_update, gradient, grad_delta, grad_pre, scaled, back_near, back_far,
):
    n = direct.shape[0]
    pick_near = picks(rows, 1 - core[0], n)
    pick_far = picks(rows, core[0], n)
    for r in blocks(n):
        total = grad_own[r, :] + dg(pick_near[r, :], near[...], 1, 0)
        total = total + dg(pick_far[r, :], far[...], 1, 0)
        gup = total.astype(BF16)
        grad_update[r, :] = gup
        grad = direct[r, :] + dg(gup, w_msg[1], 1, 1)
        gradient[r, :] = grad
        gdelta = (grad * alive_rows(count, BLOCK, r.start)).astype(BF16)
        grad_delta[r, :] = gdelta
        gpre = (dg(gdelta, w_out[0], 1, 1) * slope[r, :].astype(F32)).astype(BF16)
        grad_pre[r, :] = gpre
        scaled[r, :] = (dg(gpre, w_in[0, 1], 1, 1) * inverse[r, 0:1]).astype(BF16)
    back_near[...] = dg(a_ghost[:, 0:HALO], scaled[...], 0, 0).astype(BF16)
    back_far[...] = dg(a_ghost[:, HALO : 2 * HALO], scaled[...], 0, 0).astype(BF16)


def end_kernel(
    slabs, norm, core, rows, grad_own, near, far, direct, latents, w_msg,
    gradient, keep, give,
    gup_all, tall,
):
    n = direct.shape[0]
    total = grad_own[...] + dg(picks(rows, 1 - core[0], n), near[...], 1, 0)
    total = total + dg(picks(rows, core[0], n), far[...], 1, 0)
    gup_all[...] = total.astype(BF16)
    value = dg(latents[...], gup_all[...], 0, 0)
    pack_rows(core[0], tall, (value * norm).astype(BF16), keep, give, 0, slabs)
    gradient[...] = direct[...] + dg(gup_all[...], w_msg[0], 1, 1)


VMEM = pl.BlockSpec(memory_space=pltpu.VMEM)
SMEM = pl.BlockSpec(memory_space=pltpu.SMEM)
HBM = pl.BlockSpec(memory_space=pltpu.HBM)


def call(kernel, where, outs, scratch, gflops, limit=LIMIT):
    def run(*args):
        return pl.pallas_call(
            kernel,
            in_specs=where,
            out_specs=[VMEM] * len(outs),
            out_shape=[jax.ShapeDtypeStruct(s, d) for s, d in outs],
            scratch_shapes=scratch,
            compiler_params=pltpu.CompilerParams(vmem_limit_bytes=limit << 20),
            cost_estimate=pl.CostEstimate(
                flops=int(gflops * 1e9), transcendentals=0, bytes_accessed=int(gflops * 2e6)
            ),
        )(*args)

    return run


def reduce_rows(keep, give, slabs, bits):
    mine = keep
    for step, (here, there) in enumerate(((None, None), *bits)):
        if step:
            half = mine.reshape(2, mine.shape[0] // 2, *mine.shape[1:])
            mine, give = (
                lax.dynamic_index_in_dim(half, i, 0, keepdims=False, allow_negative_indices=False)
                for i in (here, there)
            )
        got = lax.ppermute(give, "slab", [(i, i ^ (1 << step)) for i in range(slabs)])
        mine = mine.astype(F32) + got.astype(F32)
        if step < len(bits):
            mine = mine.astype(BF16)
    return mine[0]


def body(latents, positions, counts, send_rows, tiles, w_msg, w_in, w_out, cotangent):
    n, width = latents.shape
    hidden_width = w_out.shape[1]
    slabs = lax.axis_size("slab")
    norm = 1.0 / math.sqrt(slabs * n)
    rows = send_rows[0]
    me = lax.axis_index("slab").astype(jnp.int32)
    core = (me & 1).reshape(1)
    place = [((me >> b) & 1, 1 - ((me >> b) & 1)) for b in range(1, slabs.bit_length() - 1)]
    ready = [x.reshape(1) for pair in place for x in pair] + [tiles]
    near_pairs = [(i, i ^ 1) for i in range(slabs)]
    far_pairs = [(i, i + 1 if i % 2 else i - 1) for i in range(1, slabs - 1)]

    def trade(near, far):
        far = lax.ppermute(far, "slab", far_pairs)
        near = lax.ppermute(near, "slab", near_pairs)
        return near, far

    row_b, row_f = ((n, width), BF16), ((n, width), F32)
    hid_b = ((n, hidden_width), BF16)
    halo_b = ((HALO, width), BF16)
    w_in_b = pltpu.VMEM((width, hidden_width), BF16)
    w_out_b = pltpu.VMEM((hidden_width, width), BF16)
    row_buf = pltpu.VMEM((n, width), BF16)

    near, far, latents, positions, w_msg0, w_in00 = call(
        functools.partial(send_kernel, len(ready)), [SMEM] * 2 + [VMEM] + [HBM] * 4 + [SMEM] * len(ready),
        [((HALO + GEO, width), BF16)] * 2
        + [row_b, (positions.shape, F32), ((width, width), BF16), ((width, hidden_width), BF16)],
        [pltpu.VMEM((GEO, n), F32), pltpu.SemaphoreType.DMA((4,))], 0.5, WHOLE,
    )(counts, core, rows, latents, positions, w_msg, w_in, *ready)
    near, far = trade(near, far)

    a_own, squares, columns, _, partial, pre_part = call(
        own_kernel, [SMEM] * 2 + [VMEM] * 4,
        [((n, n), BF16), ((n, TILE), F32), ((n, TILE), F32), row_b, row_f, hid_b],
        [pltpu.VMEM((TILE, n), F32), pltpu.VMEM((n // TILE, 8, TILE), F32)], 5,
    )(counts, tiles, latents, positions, w_msg0, w_in00)

    a_ghost, inverse, message0, hidden0, slope0, current1, update1, near, far = call(
        first_kernel, [SMEM] * 3 + [VMEM] * 12,
        [((n, 2 * HALO), BF16), ((n, TILE), F32), row_b, hid_b, hid_b, row_b, row_b, halo_b, halo_b],
        [pltpu.VMEM((2 * GHOST_TILES, 8, TILE), F32), pltpu.VMEM((n, TILE), F32)], 5,
    )(counts, core, tiles, rows, latents, near, far, squares, columns, partial, pre_part,
      w_msg0, w_in, w_out, w_msg)
    near, far = trade(near, far)

    partial, pre_part, grad_delta1, grad_hidden = call(
        middle_kernel, [SMEM] + [VMEM] * 6, [row_f, hid_b, row_b, hid_b], [], 3,
    )(counts, current1, update1, a_own, cotangent, w_in, w_out)

    message1, hidden1, grad_pre1, scaled1, near, far = call(
        last_kernel, [VMEM] * 8, [row_b, hid_b, hid_b, row_b, halo_b, halo_b], [], 4,
    )(near, far, a_ghost, inverse, partial, pre_part, grad_hidden, w_in)
    near, far = trade(near, far)

    out_rows, msg_rows = hidden_width // slabs, width // slabs
    in_rows = 2 * msg_rows * (hidden_width // width)

    def half(r):
        return [((slabs // 2, r, width), BF16)] * 2

    def terms(plan, heights, args):
        return call(
            functools.partial(terms_kernel, plan, slabs, norm), [SMEM] + [VMEM] * len(args),
            [o for h in heights for o in half(h)], [w_in_b, w_out_b], 4,
        )(core, *args)

    out1 = terms((((0, 1),),), (out_rows,), (hidden1, grad_delta1))
    in1 = terms((((0, 2), (1, 2)),), (in_rows,), (current1, message1, grad_pre1))
    grad_own, direct, final = call(
        flow1_kernel, [SMEM] + [VMEM] * 8, [row_f, row_f, row_b], [], 4,
    )(counts, current1, hidden1, grad_pre1, scaled1, a_own, cotangent, w_in, w_out)
    share_out1 = reduce_rows(*out1, slabs, place)
    share_in1 = reduce_rows(*in1, slabs, place)

    grad_update1, gradient1, grad_delta0, grad_pre0, scaled0, near, far = call(
        turn_kernel, [SMEM] * 2 + [VMEM] * 11,
        [row_b, row_f, row_b, hid_b, row_b, halo_b, halo_b], [], 4,
    )(counts, core, rows, grad_own, near, far, direct, slope0, inverse, a_ghost, w_msg, w_in, w_out)
    near, far = trade(near, far)

    out0 = terms((((2, 4), (3, 4)), ((5, 6), (0, 1))), (in_rows, msg_rows + out_rows),
                 (hidden0, grad_delta0, latents, message0, grad_pre0, current1, grad_update1))
    grad_own, direct = call(
        flow0_kernel, [VMEM] * 5, [row_f, row_f], [], 3,
    )(gradient1, grad_pre0, scaled0, a_own, w_in)
    share_in0 = reduce_rows(out0[0], out0[1], slabs, place)
    share_mix = reduce_rows(out0[2], out0[3], slabs, place)

    gradient, keep, give = call(
        functools.partial(end_kernel, slabs, norm), [SMEM] + [VMEM] * 7,
        [row_f] + half(msg_rows), [row_buf, w_out_b], 2,
    )(core, rows, grad_own, near, far, direct, latents, w_msg)
    share_msg0 = reduce_rows(keep, give, slabs, place)

    def unpack_in(share):
        parts = share.reshape(2, hidden_width // width, msg_rows, width)
        return jnp.concatenate([parts[:, h] for h in range(hidden_width // width)], axis=-1)

    grad_msg = jnp.stack([share_msg0, share_mix[:msg_rows]])
    grad_out = jnp.stack([share_mix[msg_rows:], share_out1])
    grad_in = jnp.stack([unpack_in(share_in0), unpack_in(share_in1)])
    return (final, gradient, grad_msg, grad_in, grad_out)


def solution(mesh):
    placed = (
        P(("groups", "slab"), None),
        P(None, ("groups", "slab")),
        P(("groups", "slab")),
        P(("groups", "slab"), None, None),
        P(("groups", "slab"), None, None),
        P(),
        P(),
        P(),
        P(("groups", "slab"), None),
    )
    return jax.shard_map(
        body,
        mesh=mesh,
        in_specs=placed,
        out_specs=(
            P(("groups", "slab"), None),
            P(("groups", "slab"), None),
            P("groups", "slab", None),
            P("groups", None, "slab", None),
            P("groups", "slab", None),
        ),
        check_vma=False,
    )
```

```python
import functools
import math

import jax
import jax.numpy as jnp
from jax import lax
from jax.experimental import pallas as pl
from jax.experimental.pallas import tpu as pltpu
from jax.sharding import PartitionSpec as P


TILE = 128
HALO = 256
GEO = 16
BLOCK = 256
LIMIT = 16
WHOLE = 50
GHOST_TILES = HALO // TILE
F32 = jnp.float32
BF16 = jnp.bfloat16


def dg(a, b, ca, cb):
    return lax.dot_general(a, b, (((ca,), (cb,)), ((), ())), preferred_element_type=F32)


def blocks(n):
    return [slice(r, r + BLOCK) for r in range(0, n, BLOCK)]


def alive_rows(count, rows, start=0):
    index = lax.broadcasted_iota(jnp.int32, (rows, 1), 0) + start
    return jnp.where(index < count[0], 1.0, 0.0).astype(F32)


def picks(rows, d, n):
    index = lax.broadcasted_iota(jnp.int32, (n, HALO), 0)
    return jnp.where(index == rows[pl.ds(d, 1), :], 1.0, 0.0).astype(BF16)


def send_kernel(scalars, count, core, rows_far, latents_far, positions_far, w_msg, w_in, *refs):
    near, far, rows, latents, positions, wm, wi, geo, sems = refs[scalars:]
    n = latents.shape[0]
    moves = (
        (positions_far, positions), (rows_far, rows), (latents_far, latents), (w_msg.at[0], wm), (w_in.at[0, 0], wi)
    )
    copies = [pltpu.make_async_copy(src, dst, sems.at[i]) for i, (src, dst) in enumerate(moves)]
    for copy in copies:
        copy.start()
    copies[0].wait()
    x = positions[...]
    high = x.astype(BF16).astype(F32)
    rest = x - high
    middle = rest.astype(BF16).astype(F32)
    geo[...] = jnp.zeros_like(geo)
    geo[0:3, :] = high
    geo[3:6, :] = middle
    geo[6:9, :] = rest - middle
    lane = lax.broadcasted_iota(jnp.int32, (1, n), 1)
    geo[9:10, :] = jnp.where(lane < count[0], 1.0, 0.0).astype(F32)
    fields = geo[...].astype(BF16)
    copies[1].wait()
    copies[2].wait()
    for d, out in ((1 - core[0], near), (core[0], far)):
        pick = picks(rows, d, n)
        out[0:HALO, :] = dg(pick, latents[...], 0, 0).astype(BF16)
        out[HALO : HALO + GEO, :] = jnp.zeros((GEO, out.shape[1]), BF16)
        out[HALO : HALO + GEO, 0:HALO] = dg(fields, pick, 1, 0).astype(BF16)
    copies[3].wait()
    copies[4].wait()


def pair_weight(x_column, geo):
    total = None
    for c in range(3):
        offset = x_column[:, c : c + 1] - geo[c : c + 1, :]
        total = offset * offset if total is None else total + offset * offset
    return geo[3:4, :] / (1.0 + total)


def own_kernel(
    count, tiles, latents, positions, wm, wi,
    a_own, squares, columns, update, partial, pre_part,
    wide, geo,
):
    n = latents.shape[0]
    tile_count = n // TILE
    wide[...] = jnp.zeros_like(wide)
    wide[0:3, :] = positions[...]
    lane = lax.broadcasted_iota(jnp.int32, (1, n), 1)
    wide[3:4, :] = jnp.where(lane < count[0], 1.0, 0.0).astype(F32)
    for t in range(tile_count):
        part = wide[:, t * TILE : (t + 1) * TILE]
        geo[t] = part[0:8]
        columns[t * TILE : (t + 1) * TILE, :] = part.T
    a_own[...] = jnp.zeros_like(a_own)
    squares[...] = jnp.zeros_like(squares)

    def tile_step(t, _):
        rows = pl.ds(pl.multiple_of(t * TILE, TILE), TILE)
        for k in range(tiles.shape[1]):
            tile = tiles[0, k, t] - GHOST_TILES

            @pl.when((tile >= 0) & (tile < tile_count))
            def _():
                weight = pair_weight(columns[rows, :], geo[tile])
                squares[rows, :] += weight * weight
                a_own[rows, pl.ds(pl.multiple_of(tile * TILE, TILE), TILE)] = weight.astype(BF16)

        return 0

    lax.fori_loop(0, tile_count, tile_step, 0)
    update[...] = dg(latents[...], wm[...], 1, 0).astype(BF16)
    partial[...] = dg(a_own[...], update[...], 1, 0)
    pre_part[...] = dg(latents[...], wi[...], 1, 0).astype(BF16)


def first_kernel(
    count, core, tiles, rows, latents, near, far, squares, columns, partial, pre_part, wm, w_in, w_out, w_msg,
    a_ghost, inverse, message, hidden, slope, current, update, send_near, send_far,
    geo, sums,
):
    n = latents.shape[0]
    tile_count = n // TILE
    for side, ghost in enumerate((near, far)):
        fields = ghost[HALO : HALO + GEO, :].astype(F32)
        place = fields[0:3] + fields[3:6] + fields[6:9]
        for g in range(GHOST_TILES):
            cut = slice(g * TILE, (g + 1) * TILE)
            geo[side * GHOST_TILES + g, 0:3, :] = place[:, cut]
            geo[side * GHOST_TILES + g, 3:4, :] = fields[9:10, cut]
    a_ghost[...] = jnp.zeros_like(a_ghost)
    sums[...] = squares[...]
    below = GHOST_TILES * (1 - core[0])
    above = GHOST_TILES * core[0] - (GHOST_TILES + tile_count)

    def tile_step(t, _):
        own = pl.ds(pl.multiple_of(t * TILE, TILE), TILE)
        for k in range(tiles.shape[1]):
            index = tiles[0, k, t]
            tile = jnp.where(index < GHOST_TILES, index + below, index + above)

            @pl.when((index < GHOST_TILES) | (index >= GHOST_TILES + tile_count))
            def _():
                weight = pair_weight(columns[own, :], geo[tile])
                sums[own, :] += weight * weight
                a_ghost[own, pl.ds(pl.multiple_of(tile * TILE, TILE), TILE)] = weight.astype(BF16)

        return 0

    lax.fori_loop(0, tile_count, tile_step, 0)
    update_near = dg(near[0:HALO, :], wm[...], 1, 0).astype(BF16)
    update_far = dg(far[0:HALO, :], wm[...], 1, 0).astype(BF16)
    for r in blocks(n):
        inv = 1.0 / jnp.sqrt(1.0 + jnp.sum(sums[r, :], axis=1, keepdims=True))
        inverse[r, :] = jnp.broadcast_to(inv, (BLOCK, TILE))
        total = partial[r, :] + dg(a_ghost[r, 0:HALO], update_near, 1, 0)
        total = total + dg(a_ghost[r, HALO : 2 * HALO], update_far, 1, 0)
        mess = (total * inv).astype(BF16)
        message[r, :] = mess
        pre = pre_part[r, :].astype(F32) + dg(mess, w_in[0, 1], 1, 0)
        sigma = 1.0 / (1.0 + jnp.exp(-pre))
        hid = (pre * sigma).astype(BF16)
        hidden[r, :] = hid
        slope[r, :] = (sigma * (1.0 + pre * (1.0 - sigma))).astype(BF16)
        delta = dg(hid, w_out[0], 1, 0)
        live = alive_rows(count, BLOCK, r.start)
        cur = (latents[r, :].astype(F32) + live * delta).astype(BF16)
        current[r, :] = cur
        update[r, :] = dg(cur, w_msg[1], 1, 0).astype(BF16)
    send_near[...] = dg(picks(rows, 1 - core[0], n), update[...], 0, 0).astype(BF16)
    send_far[...] = dg(picks(rows, core[0], n), update[...], 0, 0).astype(BF16)


def middle_kernel(
    count, current, update, a_own, cot, w_in, w_out,
    partial, pre_part, grad_delta, grad_hidden,
):
    n = current.shape[0]
    partial[...] = dg(a_own[...], update[...], 1, 0)
    pre_part[...] = dg(current[...], w_in[1, 0], 1, 0).astype(BF16)
    grad_delta[...] = (cot[...].astype(F32) * alive_rows(count, n)).astype(BF16)
    grad_hidden[...] = dg(grad_delta[...], w_out[1], 1, 1).astype(BF16)


def last_kernel(
    near, far, a_ghost, inverse, partial, pre_part, grad_hidden, w_in,
    message, hidden, grad_pre, scaled, back_near, back_far,
):
    n = partial.shape[0]
    for r in blocks(n):
        inv = inverse[r, 0:1]
        total = partial[r, :] + dg(a_ghost[r, 0:HALO], near[...], 1, 0)
        total = total + dg(a_ghost[r, HALO : 2 * HALO], far[...], 1, 0)
        mess = (total * inv).astype(BF16)
        message[r, :] = mess
        pre = pre_part[r, :].astype(F32) + dg(mess, w_in[1, 1], 1, 0)
        sigma = 1.0 / (1.0 + jnp.exp(-pre))
        hidden[r, :] = (pre * sigma).astype(BF16)
        slope = sigma * (1.0 + pre * (1.0 - sigma))
        gpre = (grad_hidden[r, :].astype(F32) * slope).astype(BF16)
        grad_pre[r, :] = gpre
        scaled[r, :] = (dg(gpre, w_in[1, 1], 1, 1) * inv).astype(BF16)
    back_near[...] = dg(a_ghost[:, 0:HALO], scaled[...], 0, 0).astype(BF16)
    back_far[...] = dg(a_ghost[:, HALO : 2 * HALO], scaled[...], 0, 0).astype(BF16)


def pack_rows(core, stage, value, keep, give, at, slabs, order):
    height, columns = value.shape
    rows, width = height // slabs, keep.shape[-1]
    stage[0:height, 0:columns] = value
    for h in range(columns // width):
        for pair in range(slabs // 2):
            place = 0
            for b in order:
                place = place * 2 + ((pair * 2 >> b) & 1)
            for out, which in ((keep, core), (give, 1 - core)):
                source = pl.ds(pl.multiple_of((pair * 2 + which) * rows, rows), rows)
                out[place, at : at + rows, :] = stage[source, h * width : (h + 1) * width]
        at += rows
    return at


def terms_kernel(plan, slabs, norm, core, *refs):
    wide, tall = refs[-2:]
    outs = refs[len(refs) - 2 - 2 * len(plan) : -2]
    for c, (order, chunk) in enumerate(plan):
        at = 0
        for a, b in chunk:
            value = (dg(refs[a][...], refs[b][...], 0, 0) * norm).astype(BF16)
            stage = tall if value.shape[1] == tall.shape[1] else wide
            at = pack_rows(core[0], stage, value, outs[2 * c], outs[2 * c + 1], at, slabs, order)


def flow1_kernel(grad_pre, scaled, a_own, cot, w_in, grad_own, direct):
    grad_own[...] = dg(a_own[...], scaled[...], 0, 0)
    direct[...] = cot[...].astype(F32) + dg(grad_pre[...], w_in[1, 0], 1, 1)


def flow0_kernel(scaled, a_own, grad_own):
    grad_own[...] = dg(a_own[...], scaled[...], 0, 0)


def turn_kernel(
    count, core, rows, grad_own, near, far, direct, slope, inverse, a_ghost, w_msg, w_in, w_out,
    grad_update, gradient, grad_delta, grad_pre, scaled, back_near, back_far,
):
    n = direct.shape[0]
    pick_near = picks(rows, 1 - core[0], n)
    pick_far = picks(rows, core[0], n)
    for r in blocks(n):
        total = grad_own[r, :] + dg(pick_near[r, :], near[...], 1, 0)
        total = total + dg(pick_far[r, :], far[...], 1, 0)
        gup = total.astype(BF16)
        grad_update[r, :] = gup
        grad = direct[r, :] + dg(gup, w_msg[1], 1, 1)
        gradient[r, :] = grad
        gdelta = (grad * alive_rows(count, BLOCK, r.start)).astype(BF16)
        grad_delta[r, :] = gdelta
        gpre = (dg(gdelta, w_out[0], 1, 1) * slope[r, :].astype(F32)).astype(BF16)
        grad_pre[r, :] = gpre
        scaled[r, :] = (dg(gpre, w_in[0, 1], 1, 1) * inverse[r, 0:1]).astype(BF16)
    back_near[...] = dg(a_ghost[:, 0:HALO], scaled[...], 0, 0).astype(BF16)
    back_far[...] = dg(a_ghost[:, HALO : 2 * HALO], scaled[...], 0, 0).astype(BF16)


def end_kernel(
    slabs, norm, order, core, rows, grad_own, near, far, latents,
    gup_all, keep, give,
    tall,
):
    n = latents.shape[0]
    total = grad_own[...] + dg(picks(rows, 1 - core[0], n), near[...], 1, 0)
    total = total + dg(picks(rows, core[0], n), far[...], 1, 0)
    gup_all[...] = total.astype(BF16)
    value = dg(latents[...], gup_all[...], 0, 0)
    pack_rows(core[0], tall, (value * norm).astype(BF16), keep, give, 0, slabs, order)


def share_kernel(plan, *refs):
    outs = refs[-3:]
    for c, pieces in enumerate(plan):
        half, here, got = refs[3 * c : 3 * c + 3]
        total = half[here[0], 0].astype(F32) + got[0].astype(F32)
        at = 0
        for o, layer, parts in pieces:
            out = outs[o]
            rows, width = out.shape[-2], total.shape[-1]
            for p in range(parts):
                for h in range(out.shape[-1] // width):
                    block = (layer, p) if len(out.shape) == 4 else (layer,)
                    out[(*block, slice(None), slice(h * width, (h + 1) * width))] = total[at : at + rows]
                    at += rows


def tail_kernel(count, gradient1, grad_pre, grad_update, current, hidden, w_msg, w_in, w_out, gradient, final):
    direct = gradient1[...] + dg(grad_pre[...], w_in[0, 0], 1, 1)
    gradient[...] = direct + dg(grad_update[...], w_msg[0], 1, 1)
    delta = dg(hidden[...], w_out[1], 1, 0)
    live = alive_rows(count, current.shape[0])
    final[...] = (current[...].astype(F32) + live * delta).astype(BF16)


VMEM = pl.BlockSpec(memory_space=pltpu.VMEM)
SMEM = pl.BlockSpec(memory_space=pltpu.SMEM)
HBM = pl.BlockSpec(memory_space=pltpu.HBM)


def call(kernel, where, outs, scratch, gflops, limit=LIMIT):
    def run(*args):
        return pl.pallas_call(
            kernel,
            in_specs=where,
            out_specs=[VMEM] * len(outs),
            out_shape=[jax.ShapeDtypeStruct(s, d) for s, d in outs],
            scratch_shapes=scratch,
            compiler_params=pltpu.CompilerParams(vmem_limit_bytes=limit << 20),
            cost_estimate=pl.CostEstimate(flops=int(gflops * 1e9), transcendentals=0, bytes_accessed=int(gflops * 2e6)),
        )(*args)

    return run


def reduce_rows(keep, give, slabs, place, order):
    mine = keep
    for step, bit in enumerate((0, *order)):
        if step:
            here, there = place[bit - 1]
            half = mine.reshape(2, mine.shape[0] // 2, *mine.shape[1:])
            take = functools.partial(lax.dynamic_index_in_dim, keepdims=False, allow_negative_indices=False)
            give = take(half, there, 0)
            mine = take(half, here, 0)
        got = lax.ppermute(give, "slab", [(i, i ^ (1 << bit)) for i in range(slabs)])
        if step == len(order):
            return half, here.reshape(1), got
        mine = (mine.astype(F32) + got.astype(F32)).astype(BF16)


def body(latents, positions, counts, send_rows, tiles, w_msg, w_in, w_out, cotangent):
    n, width = latents.shape
    hidden_width = w_out.shape[1]
    slabs = lax.axis_size("slab")
    norm = 1.0 / math.sqrt(slabs * n)
    rows = send_rows[0]
    tiles = tiles.transpose(0, 2, 1)
    me = lax.axis_index("slab").astype(jnp.int32)
    core = (me & 1).reshape(1)
    place = [((me >> b) & 1, 1 - ((me >> b) & 1)) for b in range(1, slabs.bit_length() - 1)]
    ready = [x.reshape(1) for pair in place for x in pair]
    near_pairs = [(i, i ^ 1) for i in range(slabs)]
    far_pairs = [(i, i + 1 if i % 2 else i - 1) for i in range(1, slabs - 1)]

    def trade(near, far):
        far = lax.ppermute(far, "slab", far_pairs)
        near = lax.ppermute(near, "slab", near_pairs)
        return near, far

    row_b, row_f = ((n, width), BF16), ((n, width), F32)
    hid_b = ((n, hidden_width), BF16)
    halo_b = ((HALO, width), BF16)
    w_in_b = pltpu.VMEM((width, hidden_width), BF16)
    w_out_b = pltpu.VMEM((hidden_width, width), BF16)

    near, far, rows, latents, positions, w_msg0, w_in00 = call(
        functools.partial(send_kernel, len(ready)), [SMEM] * 2 + [HBM] * 5 + [SMEM] * len(ready),
        [((HALO + GEO, width), BF16)] * 2
        + [(rows.shape, jnp.int32), row_b, (positions.shape, F32), ((width, width), BF16), ((width, hidden_width), BF16)],
        [pltpu.VMEM((GEO, n), F32), pltpu.SemaphoreType.DMA((5,))], 0.5, WHOLE,
    )(counts, core, rows, latents, positions, w_msg, w_in, *ready)
    near, far = trade(near, far)

    a_own, squares, columns, _, partial, pre_part = call(
        own_kernel, [SMEM] * 2 + [VMEM] * 4,
        [((n, n), BF16), ((n, TILE), F32), ((n, TILE), F32), row_b, row_f, hid_b],
        [pltpu.VMEM((TILE, n), F32), pltpu.VMEM((n // TILE, 8, TILE), F32)], 5,
    )(counts, tiles, latents, positions, w_msg0, w_in00)

    a_ghost, inverse, message0, hidden0, slope0, current1, update1, near, far = call(
        first_kernel, [SMEM] * 3 + [VMEM] * 12,
        [((n, 2 * HALO), BF16), ((n, TILE), F32), row_b, hid_b, hid_b, row_b, row_b, halo_b, halo_b],
        [pltpu.VMEM((2 * GHOST_TILES, 8, TILE), F32), pltpu.VMEM((n, TILE), F32)], 5,
    )(counts, core, tiles, rows, latents, near, far, squares, columns, partial, pre_part,
      w_msg0, w_in, w_out, w_msg)
    near, far = trade(near, far)

    partial, pre_part, grad_delta1, grad_hidden = call(
        middle_kernel, [SMEM] + [VMEM] * 6, [row_f, hid_b, row_b, hid_b], [], 3,
    )(counts, current1, update1, a_own, cotangent, w_in, w_out)

    message1, hidden1, grad_pre1, scaled1, near, far = call(
        last_kernel, [VMEM] * 8, [row_b, hid_b, hid_b, row_b, halo_b, halo_b], [], 4,
    )(near, far, a_ghost, inverse, partial, pre_part, grad_hidden, w_in)
    near, far = trade(near, far)

    out_rows, msg_rows = hidden_width // slabs, width // slabs
    in_rows = 2 * msg_rows * (hidden_width // width)

    def half(r):
        return [((slabs // 2, r, width), BF16)] * 2

    def terms(plan, heights, args):
        return call(
            functools.partial(terms_kernel, plan, slabs, norm), [SMEM] + [VMEM] * len(args),
            [o for h in heights for o in half(h)], [w_in_b, w_out_b], 4,
        )(core, *args)

    bits = list(range(1, slabs.bit_length() - 1))
    plain = tuple(bits)
    swapped = (2, 1, *bits[2:])
    out1 = terms(((plain, ((0, 1),)),), (out_rows,), (hidden1, grad_delta1))
    in1 = terms(((swapped, ((0, 2), (1, 2))),), (in_rows,), (current1, message1, grad_pre1))
    grad_own, direct = call(flow1_kernel, [VMEM] * 5, [row_f, row_f], [], 3)(grad_pre1, scaled1, a_own, cotangent, w_in)
    share_out1 = reduce_rows(*out1, slabs, place, plain)
    share_in1 = reduce_rows(*in1, slabs, place, swapped)

    grad_update1, gradient1, grad_delta0, grad_pre0, scaled0, near, far = call(
        turn_kernel, [SMEM] * 2 + [VMEM] * 11,
        [row_b, row_f, row_b, hid_b, row_b, halo_b, halo_b], [], 4,
    )(counts, core, rows, grad_own, near, far, direct, slope0, inverse, a_ghost, w_msg, w_in, w_out)
    near, far = trade(near, far)

    out0 = terms(((plain, ((2, 4), (3, 4))), (swapped, ((5, 6), (0, 1)))), (in_rows, msg_rows + out_rows),
                 (hidden0, grad_delta0, latents, message0, grad_pre0, current1, grad_update1))
    (grad_own,) = call(flow0_kernel, [VMEM] * 2, [row_f], [], 2)(scaled0, a_own)
    share_in0 = reduce_rows(*out0[:2], slabs, place, plain)
    share_mix = reduce_rows(*out0[2:], slabs, place, swapped)

    grad_update0, keep, give = call(
        functools.partial(end_kernel, slabs, norm, plain), [SMEM] + [VMEM] * 5,
        [row_b] + half(msg_rows), [w_out_b], 2,
    )(core, rows, grad_own, near, far, latents)
    share_msg0 = reduce_rows(keep, give, slabs, place, plain)

    gradient, final = call(
        tail_kernel, [SMEM] + [VMEM] * 8, [row_f, row_b], [], 4,
    )(counts, gradient1, grad_pre0, grad_update0, current1, hidden1, w_msg, w_in, w_out)

    plan = (((2, 1, 1),), ((1, 1, 2),), ((1, 0, 2),), ((0, 1, 1), (2, 0, 1)), ((0, 0, 1),))
    grad_msg, grad_in, grad_out = call(
        functools.partial(share_kernel, plan), [VMEM, SMEM, VMEM] * len(plan),
        [((2, msg_rows, width), F32), ((2, 2, msg_rows, hidden_width), F32), ((2, out_rows, width), F32)], [], 0.1,
    )(*share_out1, *share_in1, *share_in0, *share_mix, *share_msg0)
    return (final, gradient, grad_msg, grad_in, grad_out)


def solution(mesh):
    placed = (
        P(("groups", "slab"), None),
        P(None, ("groups", "slab")),
        P(("groups", "slab")),
        P(("groups", "slab"), None, None),
        P(("groups", "slab"), None, None),
        P(),
        P(),
        P(),
        P(("groups", "slab"), None),
    )
    return jax.shard_map(
        body,
        mesh=mesh,
        in_specs=placed,
        out_specs=(
            P(("groups", "slab"), None),
            P(("groups", "slab"), None),
            P("groups", "slab", None),
            P("groups", None, "slab", None),
            P("groups", "slab", None),
        ),
        check_vma=False,
    )
```

```python
import functools
import math

import jax
import jax.numpy as jnp
from jax import lax
from jax.experimental import pallas as pl
from jax.experimental.pallas import tpu as pltpu
from jax.sharding import PartitionSpec as P


TILE = 128
HALO = 256
GEO = 16
BLOCK = 1024
LIMIT = 16
WHOLE = 50
GHOST_TILES = HALO // TILE
F32 = jnp.float32
BF16 = jnp.bfloat16


def dg(a, b, ca, cb):
    return lax.dot_general(a, b, (((ca,), (cb,)), ((), ())), preferred_element_type=F32)


def blocks(n):
    return [slice(r, r + BLOCK) for r in range(0, n, BLOCK)]


def alive_rows(count, rows, start=0):
    index = lax.broadcasted_iota(jnp.int32, (rows, 1), 0) + start
    return jnp.where(index < count[0], 1.0, 0.0).astype(F32)


def picks(rows, d, n):
    index = lax.broadcasted_iota(jnp.int32, (n, HALO), 0)
    return jnp.where(index == rows[pl.ds(d, 1), :], 1.0, 0.0).astype(BF16)


def send_kernel(scalars, count, core, rows_far, latents_far, positions_far, w_msg, w_in, *refs):
    near, far, rows, latents, positions, wm, wi, geo, sems = refs[scalars:]
    n = latents.shape[0]
    moves = (
        (positions_far, positions), (rows_far, rows), (latents_far, latents), (w_msg.at[0], wm), (w_in.at[0, 0], wi)
    )
    copies = [pltpu.make_async_copy(src, dst, sems.at[i]) for i, (src, dst) in enumerate(moves)]
    for copy in copies:
        copy.start()
    copies[0].wait()
    x = positions[...]
    high = x.astype(BF16).astype(F32)
    rest = x - high
    middle = rest.astype(BF16).astype(F32)
    geo[...] = jnp.zeros_like(geo)
    geo[0:3, :] = high
    geo[3:6, :] = middle
    geo[6:9, :] = rest - middle
    lane = lax.broadcasted_iota(jnp.int32, (1, n), 1)
    geo[9:10, :] = jnp.where(lane < count[0], 1.0, 0.0).astype(F32)
    fields = geo[...].astype(BF16)
    copies[1].wait()
    copies[2].wait()
    for d, out in ((1 - core[0], near), (core[0], far)):
        pick = picks(rows, d, n)
        out[0:HALO, :] = dg(pick, latents[...], 0, 0).astype(BF16)
        out[HALO : HALO + GEO, :] = jnp.zeros((GEO, out.shape[1]), BF16)
        out[HALO : HALO + GEO, 0:HALO] = dg(fields, pick, 1, 0).astype(BF16)
    copies[3].wait()
    copies[4].wait()


def pair_weight(x_column, geo):
    total = None
    for c in range(3):
        offset = x_column[:, c : c + 1] - geo[c : c + 1, :]
        total = offset * offset if total is None else total + offset * offset
    return geo[3:4, :] / (1.0 + total)


def own_kernel(
    count, tiles, latents, positions, wm, wi,
    a_own, squares, columns, update, partial, pre_part,
    wide, geo,
):
    n = latents.shape[0]
    tile_count = n // TILE
    wide[...] = jnp.zeros_like(wide)
    wide[0:3, :] = positions[...]
    lane = lax.broadcasted_iota(jnp.int32, (1, n), 1)
    wide[3:4, :] = jnp.where(lane < count[0], 1.0, 0.0).astype(F32)
    for t in range(tile_count):
        part = wide[:, t * TILE : (t + 1) * TILE]
        geo[t] = part[0:8]
        columns[t * TILE : (t + 1) * TILE, :] = part.T
    a_own[...] = jnp.zeros_like(a_own)
    squares[...] = jnp.zeros_like(squares)

    def tile_step(t, _):
        rows = pl.ds(pl.multiple_of(t * TILE, TILE), TILE)
        for k in range(tiles.shape[1]):
            tile = tiles[0, k, t] - GHOST_TILES

            @pl.when((tile >= 0) & (tile < tile_count))
            def _():
                weight = pair_weight(columns[rows, :], geo[tile])
                squares[rows, :] += weight * weight
                a_own[rows, pl.ds(pl.multiple_of(tile * TILE, TILE), TILE)] = weight.astype(BF16)

        return 0

    lax.fori_loop(0, tile_count, tile_step, 0)
    update[...] = dg(latents[...], wm[...], 1, 0).astype(BF16)
    partial[...] = dg(a_own[...], update[...], 1, 0)
    pre_part[...] = dg(latents[...], wi[...], 1, 0).astype(BF16)


def first_kernel(
    count, core, tiles, rows, latents, near, far, squares, columns, partial, pre_part, wm, w_in, w_out, w_msg,
    a_ghost, inverse, message, hidden, slope, current, update, send_near, send_far,
    geo, sums,
):
    n = latents.shape[0]
    tile_count = n // TILE
    for side, ghost in enumerate((near, far)):
        fields = ghost[HALO : HALO + GEO, :].astype(F32)
        place = fields[0:3] + fields[3:6] + fields[6:9]
        for g in range(GHOST_TILES):
            cut = slice(g * TILE, (g + 1) * TILE)
            geo[side * GHOST_TILES + g, 0:3, :] = place[:, cut]
            geo[side * GHOST_TILES + g, 3:4, :] = fields[9:10, cut]
    a_ghost[...] = jnp.zeros_like(a_ghost)
    sums[...] = squares[...]
    below = GHOST_TILES * (1 - core[0])
    above = GHOST_TILES * core[0] - (GHOST_TILES + tile_count)

    def tile_step(t, _):
        own = pl.ds(pl.multiple_of(t * TILE, TILE), TILE)
        for k in range(tiles.shape[1]):
            index = tiles[0, k, t]
            tile = jnp.where(index < GHOST_TILES, index + below, index + above)

            @pl.when((index < GHOST_TILES) | (index >= GHOST_TILES + tile_count))
            def _():
                weight = pair_weight(columns[own, :], geo[tile])
                sums[own, :] += weight * weight
                a_ghost[own, pl.ds(pl.multiple_of(tile * TILE, TILE), TILE)] = weight.astype(BF16)

        return 0

    lax.fori_loop(0, tile_count, tile_step, 0)
    update_near = dg(near[0:HALO, :], wm[...], 1, 0).astype(BF16)
    update_far = dg(far[0:HALO, :], wm[...], 1, 0).astype(BF16)
    for r in blocks(n):
        inv = 1.0 / jnp.sqrt(1.0 + jnp.sum(sums[r, :], axis=1, keepdims=True))
        inverse[r, :] = jnp.broadcast_to(inv, (BLOCK, TILE))
        total = partial[r, :] + dg(a_ghost[r, 0:HALO], update_near, 1, 0)
        total = total + dg(a_ghost[r, HALO : 2 * HALO], update_far, 1, 0)
        mess = (total * inv).astype(BF16)
        message[r, :] = mess
        pre = pre_part[r, :].astype(F32) + dg(mess, w_in[0, 1], 1, 0)
        sigma = 1.0 / (1.0 + jnp.exp(-pre))
        hid = (pre * sigma).astype(BF16)
        hidden[r, :] = hid
        slope[r, :] = (sigma * (1.0 + pre * (1.0 - sigma))).astype(BF16)
        delta = dg(hid, w_out[0], 1, 0)
        live = alive_rows(count, BLOCK, r.start)
        cur = (latents[r, :].astype(F32) + live * delta).astype(BF16)
        current[r, :] = cur
        update[r, :] = dg(cur, w_msg[1], 1, 0).astype(BF16)
    send_near[...] = dg(picks(rows, 1 - core[0], n), update[...], 0, 0).astype(BF16)
    send_far[...] = dg(picks(rows, core[0], n), update[...], 0, 0).astype(BF16)


def middle_kernel(
    count, current, update, a_own, cot, w_in, w_out,
    partial, pre_part, grad_delta, grad_hidden,
):
    n = current.shape[0]
    partial[...] = dg(a_own[...], update[...], 1, 0)
    pre_part[...] = dg(current[...], w_in[1, 0], 1, 0).astype(BF16)
    grad_delta[...] = (cot[...].astype(F32) * alive_rows(count, n)).astype(BF16)
    grad_hidden[...] = dg(grad_delta[...], w_out[1], 1, 1).astype(BF16)


def last_kernel(
    near, far, a_ghost, inverse, partial, pre_part, grad_hidden, w_in,
    message, hidden, grad_pre, scaled, back_near, back_far,
):
    n = partial.shape[0]
    for r in blocks(n):
        inv = inverse[r, 0:1]
        total = partial[r, :] + dg(a_ghost[r, 0:HALO], near[...], 1, 0)
        total = total + dg(a_ghost[r, HALO : 2 * HALO], far[...], 1, 0)
        mess = (total * inv).astype(BF16)
        message[r, :] = mess
        pre = pre_part[r, :].astype(F32) + dg(mess, w_in[1, 1], 1, 0)
        sigma = 1.0 / (1.0 + jnp.exp(-pre))
        hidden[r, :] = (pre * sigma).astype(BF16)
        slope = sigma * (1.0 + pre * (1.0 - sigma))
        gpre = (grad_hidden[r, :].astype(F32) * slope).astype(BF16)
        grad_pre[r, :] = gpre
        scaled[r, :] = (dg(gpre, w_in[1, 1], 1, 1) * inv).astype(BF16)
    back_near[...] = dg(a_ghost[:, 0:HALO], scaled[...], 0, 0).astype(BF16)
    back_far[...] = dg(a_ghost[:, HALO : 2 * HALO], scaled[...], 0, 0).astype(BF16)


def pack_rows(core, stage, value, keep, give, at, slabs, order):
    height, columns = value.shape
    rows, width = height // slabs, keep.shape[-1]
    stage[0:height, 0:columns] = value
    for h in range(columns // width):
        for pair in range(slabs // 2):
            place = 0
            for b in order:
                place = place * 2 + ((pair * 2 >> b) & 1)
            for out, which in ((keep, core), (give, 1 - core)):
                source = pl.ds(pl.multiple_of((pair * 2 + which) * rows, rows), rows)
                out[place, at : at + rows, :] = stage[source, h * width : (h + 1) * width]
        at += rows
    return at


def terms_kernel(plan, slabs, norm, core, *refs):
    wide, tall = refs[-2:]
    outs = refs[len(refs) - 2 - 2 * len(plan) : -2]
    for c, (order, chunk) in enumerate(plan):
        at = 0
        for a, b in chunk:
            value = (dg(refs[a][...], refs[b][...], 0, 0) * norm).astype(BF16)
            stage = tall if value.shape[1] == tall.shape[1] else wide
            at = pack_rows(core[0], stage, value, outs[2 * c], outs[2 * c + 1], at, slabs, order)


def flow1_kernel(grad_pre, scaled, a_own, cot, w_in, grad_own, direct):
    grad_own[...] = dg(a_own[...], scaled[...], 0, 0)
    direct[...] = cot[...].astype(F32) + dg(grad_pre[...], w_in[1, 0], 1, 1)


def turn_kernel(
    count, core, rows, grad_own, near, far, direct, slope, inverse, a_ghost, w_msg, w_in, w_out,
    grad_update, gradient, grad_delta, grad_pre, scaled, back_near, back_far,
):
    n = direct.shape[0]
    pick_near = picks(rows, 1 - core[0], n)
    pick_far = picks(rows, core[0], n)
    for r in blocks(n):
        total = grad_own[r, :] + dg(pick_near[r, :], near[...], 1, 0)
        total = total + dg(pick_far[r, :], far[...], 1, 0)
        gup = total.astype(BF16)
        grad_update[r, :] = gup
        grad = direct[r, :] + dg(gup, w_msg[1], 1, 1)
        gradient[r, :] = grad
        gdelta = (grad * alive_rows(count, BLOCK, r.start)).astype(BF16)
        grad_delta[r, :] = gdelta
        gpre = (dg(gdelta, w_out[0], 1, 1) * slope[r, :].astype(F32)).astype(BF16)
        grad_pre[r, :] = gpre
        scaled[r, :] = (dg(gpre, w_in[0, 1], 1, 1) * inverse[r, 0:1]).astype(BF16)
    back_near[...] = dg(a_ghost[:, 0:HALO], scaled[...], 0, 0).astype(BF16)
    back_far[...] = dg(a_ghost[:, HALO : 2 * HALO], scaled[...], 0, 0).astype(BF16)


def mix_kernel(
    slabs, norm, order, core, scaled, a_own, latents, ghost_near, ghost_far, back_near, back_far,
    later, later_update, hidden, grad_delta,
    grad_own, keep, give,
    own, tall,
):
    grad_own[...] = dg(a_own[...], scaled[...], 0, 0)
    own[...] = grad_own[...].astype(BF16)
    value = dg(latents[...], own[...], 0, 0)
    value = value + dg(ghost_near[0:HALO, :], back_near[...], 0, 0)
    value = value + dg(ghost_far[0:HALO, :], back_far[...], 0, 0)
    at = pack_rows(core[0], tall, (value * norm).astype(BF16), keep, give, 0, slabs, order)
    value = dg(later[...], later_update[...], 0, 0)
    at = pack_rows(core[0], tall, (value * norm).astype(BF16), keep, give, at, slabs, order)
    value = dg(hidden[...], grad_delta[...], 0, 0)
    pack_rows(core[0], tall, (value * norm).astype(BF16), keep, give, at, slabs, order)


def rest_kernel(count, gradient1, grad_pre, current, hidden, w_in, w_out, direct, final):
    direct[...] = gradient1[...] + dg(grad_pre[...], w_in[0, 0], 1, 1)
    delta = dg(hidden[...], w_out[1], 1, 0)
    live = alive_rows(count, current.shape[0])
    final[...] = (current[...].astype(F32) + live * delta).astype(BF16)


def end_kernel(core, rows, grad_own, near, far, direct, w_msg, gradient):
    n = direct.shape[0]
    total = grad_own[...] + dg(picks(rows, 1 - core[0], n), near[...], 1, 0)
    total = total + dg(picks(rows, core[0], n), far[...], 1, 0)
    gradient[...] = direct[...] + dg(total.astype(BF16), w_msg[0], 1, 1)


def share_kernel(plan, *refs):
    outs = refs[-3:]
    for c, pieces in enumerate(plan):
        half, here, got = refs[3 * c : 3 * c + 3]
        total = half[here[0], 0].astype(F32) + got[0].astype(F32)
        at = 0
        for o, layer, parts in pieces:
            out = outs[o]
            rows, width = out.shape[-2], total.shape[-1]
            for p in range(parts):
                for h in range(out.shape[-1] // width):
                    block = (layer, p) if len(out.shape) == 4 else (layer,)
                    out[(*block, slice(None), slice(h * width, (h + 1) * width))] = total[at : at + rows]
                    at += rows


VMEM = pl.BlockSpec(memory_space=pltpu.VMEM)
SMEM = pl.BlockSpec(memory_space=pltpu.SMEM)
HBM = pl.BlockSpec(memory_space=pltpu.HBM)


def call(kernel, where, outs, scratch, gflops, limit=LIMIT):
    def run(*args):
        return pl.pallas_call(
            kernel,
            in_specs=where,
            out_specs=[VMEM] * len(outs),
            out_shape=[jax.ShapeDtypeStruct(s, d) for s, d in outs],
            scratch_shapes=scratch,
            compiler_params=pltpu.CompilerParams(vmem_limit_bytes=limit << 20),
            cost_estimate=pl.CostEstimate(flops=int(gflops * 1e9), transcendentals=0, bytes_accessed=int(gflops * 2e6)),
        )(*args)

    return run


def reduce_rows(keep, give, slabs, place, order):
    mine = keep
    for step, bit in enumerate((0, *order)):
        if step:
            here, there = place[bit - 1]
            half = mine.reshape(2, mine.shape[0] // 2, *mine.shape[1:])
            take = functools.partial(lax.dynamic_index_in_dim, keepdims=False, allow_negative_indices=False)
            give = take(half, there, 0)
            mine = take(half, here, 0)
        got = lax.ppermute(give, "slab", [(i, i ^ (1 << bit)) for i in range(slabs)])
        if step == len(order):
            return half, here.reshape(1), got
        mine = (mine.astype(F32) + got.astype(F32)).astype(BF16)


def body(latents, positions, counts, send_rows, tiles, w_msg, w_in, w_out, cotangent):
    n, width = latents.shape
    hidden_width = w_out.shape[1]
    slabs = lax.axis_size("slab")
    norm = 1.0 / math.sqrt(slabs * n)
    rows = send_rows[0]
    tiles = tiles.transpose(0, 2, 1)
    me = lax.axis_index("slab").astype(jnp.int32)
    core = (me & 1).reshape(1)
    place = [((me >> b) & 1, 1 - ((me >> b) & 1)) for b in range(1, slabs.bit_length() - 1)]
    ready = [x.reshape(1) for pair in place for x in pair]
    near_pairs = [(i, i ^ 1) for i in range(slabs)]
    far_pairs = [(i, i + 1 if i % 2 else i - 1) for i in range(1, slabs - 1)]

    def trade(near, far):
        far = lax.ppermute(far, "slab", far_pairs)
        near = lax.ppermute(near, "slab", near_pairs)
        return near, far

    row_b, row_f = ((n, width), BF16), ((n, width), F32)
    hid_b = ((n, hidden_width), BF16)
    halo_b = ((HALO, width), BF16)
    w_in_b = pltpu.VMEM((width, hidden_width), BF16)
    w_out_b = pltpu.VMEM((hidden_width, width), BF16)

    near, far, rows, latents, positions, w_msg0, w_in00 = call(
        functools.partial(send_kernel, len(ready)), [SMEM] * 2 + [HBM] * 5 + [SMEM] * len(ready),
        [((HALO + GEO, width), BF16)] * 2
        + [(rows.shape, jnp.int32), row_b, (positions.shape, F32), ((width, width), BF16), ((width, hidden_width), BF16)],
        [pltpu.VMEM((GEO, n), F32), pltpu.SemaphoreType.DMA((5,))], 0.5, WHOLE,
    )(counts, core, rows, latents, positions, w_msg, w_in, *ready)
    near, far = trade(near, far)
    ghost_near, ghost_far = near, far

    a_own, squares, columns, _, partial, pre_part = call(
        own_kernel, [SMEM] * 2 + [VMEM] * 4,
        [((n, n), BF16), ((n, TILE), F32), ((n, TILE), F32), row_b, row_f, hid_b],
        [pltpu.VMEM((TILE, n), F32), pltpu.VMEM((n // TILE, 8, TILE), F32)], 5,
    )(counts, tiles, latents, positions, w_msg0, w_in00)

    a_ghost, inverse, message0, hidden0, slope0, current1, update1, near, far = call(
        first_kernel, [SMEM] * 3 + [VMEM] * 12,
        [((n, 2 * HALO), BF16), ((n, TILE), F32), row_b, hid_b, hid_b, row_b, row_b, halo_b, halo_b],
        [pltpu.VMEM((2 * GHOST_TILES, 8, TILE), F32), pltpu.VMEM((n, TILE), F32)], 5,
    )(counts, core, tiles, rows, latents, near, far, squares, columns, partial, pre_part,
      w_msg0, w_in, w_out, w_msg)
    near, far = trade(near, far)

    partial, pre_part, grad_delta1, grad_hidden = call(
        middle_kernel, [SMEM] + [VMEM] * 6, [row_f, hid_b, row_b, hid_b], [], 3,
    )(counts, current1, update1, a_own, cotangent, w_in, w_out)

    message1, hidden1, grad_pre1, scaled1, near, far = call(
        last_kernel, [VMEM] * 8, [row_b, hid_b, hid_b, row_b, halo_b, halo_b], [], 4,
    )(near, far, a_ghost, inverse, partial, pre_part, grad_hidden, w_in)
    near, far = trade(near, far)

    out_rows, msg_rows = hidden_width // slabs, width // slabs
    in_rows = 2 * msg_rows * (hidden_width // width)

    def half(r):
        return [((slabs // 2, r, width), BF16)] * 2

    def terms(plan, heights, args):
        return call(
            functools.partial(terms_kernel, plan, slabs, norm), [SMEM] + [VMEM] * len(args),
            [o for h in heights for o in half(h)], [w_in_b, w_out_b], 4,
        )(core, *args)

    bits = list(range(1, slabs.bit_length() - 1))
    plain = tuple(bits)
    swapped = (2, 1, *bits[2:])
    out1 = terms(((plain, ((0, 1),)),), (out_rows,), (hidden1, grad_delta1))
    in1 = terms(((swapped, ((0, 2), (1, 2))),), (in_rows,), (current1, message1, grad_pre1))
    grad_own, direct = call(flow1_kernel, [VMEM] * 5, [row_f, row_f], [], 3)(grad_pre1, scaled1, a_own, cotangent, w_in)
    share_out1 = reduce_rows(*out1, slabs, place, plain)
    share_in1 = reduce_rows(*in1, slabs, place, swapped)

    grad_update1, gradient1, grad_delta0, grad_pre0, scaled0, near, far = call(
        turn_kernel, [SMEM] * 2 + [VMEM] * 11,
        [row_b, row_f, row_b, hid_b, row_b, halo_b, halo_b], [], 4,
    )(counts, core, rows, grad_own, near, far, direct, slope0, inverse, a_ghost, w_msg, w_in, w_out)
    back_near, back_far = near, far
    near, far = trade(near, far)

    in0 = terms(((plain, ((0, 2), (1, 2))),), (in_rows,), (latents, message0, grad_pre0))
    grad_own, *mix0 = call(
        functools.partial(mix_kernel, slabs, norm, swapped), [SMEM] + [VMEM] * 11,
        [row_f] + half(2 * msg_rows + out_rows), [pltpu.VMEM((n, width), BF16), w_out_b], 5,
    )(core, scaled0, a_own, latents, ghost_near, ghost_far, back_near, back_far,
      current1, grad_update1, hidden0, grad_delta0)
    direct, final = call(
        rest_kernel, [SMEM] + [VMEM] * 6, [row_f, row_b], [], 3,
    )(counts, gradient1, grad_pre0, current1, hidden1, w_in, w_out)
    (gradient,) = call(end_kernel, [SMEM] + [VMEM] * 6, [row_f], [], 2)(core, rows, grad_own, near, far, direct, w_msg)
    share_in0 = reduce_rows(*in0, slabs, place, plain)
    share_mix = reduce_rows(*mix0, slabs, place, swapped)

    plan = (((2, 1, 1),), ((1, 1, 2),), ((1, 0, 2),), ((0, 0, 1), (0, 1, 1), (2, 0, 1)))
    grad_msg, grad_in, grad_out = call(
        functools.partial(share_kernel, plan), [VMEM, SMEM, VMEM] * len(plan),
        [((2, msg_rows, width), F32), ((2, 2, msg_rows, hidden_width), F32), ((2, out_rows, width), F32)], [], 0.1,
    )(*share_out1, *share_in1, *share_in0, *share_mix)
    return (final, gradient, grad_msg, grad_in, grad_out)


def solution(mesh):
    placed = (
        P(("groups", "slab"), None),
        P(None, ("groups", "slab")),
        P(("groups", "slab")),
        P(("groups", "slab"), None, None),
        P(("groups", "slab"), None, None),
        P(),
        P(),
        P(),
        P(("groups", "slab"), None),
    )
    return jax.shard_map(
        body,
        mesh=mesh,
        in_specs=placed,
        out_specs=(
            P(("groups", "slab"), None),
            P(("groups", "slab"), None),
            P("groups", "slab", None),
            P("groups", None, "slab", None),
            P("groups", "slab", None),
        ),
        check_vma=False,
    )
```
